32 devices in a mesh: dp: 2 (over y), ctx: 8 (over z, x), segment: 2 (over core).
Axes of the slice: x: 2, y: 2, z: 4, core: 2. Of those that a mesh axis runs over, the one named last changes fastest.
Arguments:
- inputs: bfloat16 [2, 2048, 1536], P('dp', 'ctx'), may hold values from -6 to 6
- cotangent: bfloat16 [2, 2048, 1536], P('dp', 'ctx'), may hold values from -6 to 6
- weights: bfloat16 [2, 1536, 1536], P('segment', 'ctx'), may hold values from -0.15625 to 0.15625
- tap_weights: float32 [2, 3, 1536], P('segment'), may hold values from -3 to 3
- projection: bfloat16 [2, 1536, 256], P('segment'), may hold values from -0.15625 to 0.15625
- dilations: int32 [2], replicated, may hold values from 1 to 64, as said below
Outputs:
- input_grad: bfloat16 [2, 2048, 1536], P('dp', 'ctx', 'segment')
- sketches: float32 [2, 256, 1536], P('segment', 'ctx')
The draws below stay inside these ranges and needn't reach their ends.
Inputs may be any that keep to these rules, and one draw needn't show every extreme that they name: `dilations`: each entry is a section's dilation; one of the two equals 64.
All inputs are finite; a program needn't handle non-finite values.
Results may differ from the reference program's by a relative error of at most 0.02.
Values may be sent and summed in bfloat16 or wider, within the bound.
A program may use at most 64 MiB of HBM per device.

```python
import jax
import jax.numpy as jnp
from jax import lax

C = 1536
K = 256
DMAX = 64
BATCH = 2
LENGTH = 2048


def draw_dilations(key, part):
    first_key, second_key = jax.random.split(jax.random.fold_in(key, 17))
    values = jax.random.randint(first_key, (2,), 1, DMAX + 1)
    which = jax.random.randint(second_key, (), 0, 2)
    return jnp.where(jnp.arange(2) == which, DMAX, values).astype(jnp.int32)


def with_spikes(result, stream_key, source, target, blocks, factor):
    owner, partner = [(jnp.arange(result.shape[axis_at]) // (result.shape[axis_at] // blocks)).reshape([-1 if axis == axis_at else 1 for axis in range(result.ndim)]) for axis_at in (source, target)]
    chosen = jax.random.permutation(stream_key, blocks)[partner]
    strong = (owner == chosen) | (owner == (partner + blocks // 2) % blocks)
    return jnp.where(strong, factor * result, result)


def shard_levels(rng, shape, pieces, low, largest):
    def one(position, parts):
        heights = jax.random.uniform(jax.random.fold_in(jax.random.fold_in(rng, 6), position), (parts,), jnp.float32, low / len(pieces), largest / len(pieces))
        return jnp.repeat(jnp.exp(heights), shape[position] // parts).reshape((-1,) + (1,) * (len(shape) - position - 1))

    loudness = one(*pieces[0])
    for cut in pieces[1:]:
        loudness = loudness * one(*cut)
    return loudness


def normal_values(rng, extent, deviation, bound, cuts=(), held_as=jnp.bfloat16):
    values = jax.random.normal(rng, extent, jnp.float32) * deviation
    if len(cuts) > 0:
        values = shard_levels(rng, extent, cuts, -0.22, 0.18) * values
    return jnp.clip(values, min=-bound, max=bound).astype(held_as)


def noise_with(stream_key, shape, width, limit, shards, heavy, dtype=jnp.bfloat16):
    drawn = width * jax.random.normal(stream_key, shape, jnp.float32)
    if shards:
        drawn = drawn * shard_levels(stream_key, shape, shards, -0.22, 0.18)
    return jnp.clip(with_spikes(drawn, jax.random.fold_in(stream_key, 3), *heavy), -limit, limit).astype(dtype)


def setup_inputs(seed: int = 0) -> dict:
    keys = jax.random.split(jax.random.key(seed), 7)
    return {
        "inputs": normal_values(keys[0], (BATCH, LENGTH, C), 1.0, 6.0, ((0, 2), (1, 8))),
        "cotangent": noise_with(keys[1], (BATCH, LENGTH, C), 1.0, 6.0, ((0, 2), (1, 8)), (1, 2, 8, 2.0)),
        "weights": normal_values(keys[2], (2, C, C), C ** -0.5, 0.15625, ((0, 2), (1, 8))),
        "tap_weights": normal_values(keys[3], (2, 3, C), 0.6, 3.0, ((0, 2),), jnp.float32),
        "projection": normal_values(keys[4], (2, C, K), C ** -0.5, 0.15625, ((0, 2),)),
        "dilations": draw_dilations(jax.random.fold_in(keys[6], 71), 0),
    }


def activate(values):
    normed = values * lax.rsqrt(lax.optimization_barrier(jnp.mean(values * values, axis=-1, keepdims=True)) + 1e-06)
    return jax.nn.gelu(normed, approximate=True)

def shifted(values, offset):
    padded = jnp.pad(values, ((DMAX, DMAX), (0, 0)))
    start = (DMAX + offset).astype(jnp.int32)
    return lax.dynamic_slice_in_dim(padded, start, values.shape[0], 0)

def mix(rows, taps, dilation):
    activated = activate(rows.astype(jnp.float32)).astype(jnp.bfloat16)
    mixed = taps[0] * shifted(activated, -dilation) + taps[1] * activated + taps[2] * shifted(activated, dilation)
    return mixed.astype(jnp.bfloat16)

def backward(rows, grad, matrix, taps, projection, dilation):
    mixed = mix(rows, taps, dilation)
    grad_mixed = jnp.dot(grad, matrix.T, preferred_element_type=jnp.float32).astype(jnp.bfloat16)
    grad_act = taps[0] * shifted(grad_mixed, dilation) + taps[1] * grad_mixed + taps[2] * shifted(grad_mixed, -dilation)
    primal, pullback = jax.vjp(activate, rows.astype(jnp.float32))
    grad_rows = pullback(grad_act)[0]
    grad_in = (grad.astype(jnp.float32) + grad_rows).astype(jnp.bfloat16)
    sketched = jnp.dot(grad, projection, preferred_element_type=jnp.float32).astype(jnp.bfloat16)
    sketch = jnp.dot(sketched.T, mixed, preferred_element_type=jnp.float32)
    return (grad_in, sketch)

def reference(inputs, cotangent, weights, tap_weights, projection, dilations):
    first = dilations[0]
    second = dilations[1]

    def one_sequence(pair):
        rows, grad_out = pair
        mixed = mix(rows, tap_weights[0], first)
        middle = (rows.astype(jnp.float32) + jnp.dot(mixed, weights[0], preferred_element_type=jnp.float32)).astype(jnp.bfloat16)
        grad_middle, sketch_late = backward(middle, grad_out, weights[1], tap_weights[1], projection[1], second)
        grad_input, sketch_early = backward(rows, grad_middle, weights[0], tap_weights[0], projection[0], first)
        return (grad_input, sketch_early, sketch_late)
    grad_input, sketch_early, sketch_late = lax.map(one_sequence, (inputs, cotangent))
    sketches = jnp.stack([lax.optimization_barrier(jnp.sum(sketch_early, axis=0)), lax.optimization_barrier(jnp.sum(sketch_late, axis=0))])
    return (grad_input, sketches)
```

```python
import functools

import jax
import jax.numpy as jnp
from jax import lax
from jax.experimental import pallas as pl
from jax.experimental.pallas import tpu as pltpu
from jax.sharding import PartitionSpec as P

DMAX = 64
MESH = pl.DeviceIdType.MESH
F32 = jnp.float32
BF16 = jnp.bfloat16
ROOT = 0.7978845608028654
CUBIC = 0.044715


def line_width(n):
    width = 1
    while 4 * width * width <= n:
        width *= 2
    return width


def kernel(
    n, m, x_ref, g_ref, w_ref, tap_ref, proj_ref, dil_ref, out_ref, sk_ref,
    wf, act, halo_a, halo_g, mixed, gu, ga, first, second, other, sk, rs, dpb, pb,
    w_send, w_recv, h_send, h_recv, c_send, c_recv, rs_send, rs_recv, dp_send, dp_recv,
):
    me = lax.axis_index("ctx")
    dp = lax.axis_index("dp")
    seg = lax.axis_index("segment")
    length, width = x_ref.shape
    rows = w_ref.shape[0]
    kr = sk.shape[1]
    X = line_width(n)
    Z = n // X
    z = me // X
    x = lax.rem(me, X)
    crossing = m % 2 == 0 and rows % 48 == 0
    parts = 2 if crossing else 1
    pr = rows // 3 if crossing else rows
    q = lax.rem(dp, 2) if crossing else 0

    barrier = pltpu.get_barrier_semaphore()
    for k in range(1, n):
        pl.semaphore_signal(barrier, inc=1, device_id={"ctx": lax.rem(me + k, n)}, device_id_type=MESH)
    for k in range(1, m):
        pl.semaphore_signal(barrier, inc=1, device_id={"dp": lax.rem(dp + k, m)}, device_id_type=MESH)
    pl.semaphore_signal(barrier, inc=1, device_id={"segment": 1 - seg}, device_id_type=MESH)
    pl.semaphore_wait(barrier, n + m - 1)

    def piece(block, part):
        return pl.ds(pl.multiple_of(block * rows + part * pr, 16), pr)

    def w_copy(block, part, direction, where, own=False):
        src = w_ref.at[pl.ds(pl.multiple_of(part * pr, 16), pr)] if own else wf.at[piece(block, part)]
        return pltpu.make_async_remote_copy(
            src_ref=src,
            dst_ref=wf.at[piece(block, part)],
            send_sem=w_send.at[block, part, direction],
            recv_sem=w_recv.at[block, part],
            device_id=where,
            device_id_type=MESH,
        )

    def sends_z(block, part, up, own=False):
        if up:
            return (z < Z - 1, lambda: w_copy(block, part, 0, {"ctx": me + X}, own))
        return (z > 0, lambda: w_copy(block, part, 1, {"ctx": me - X}, own))

    def sends_x(block, part, right, own=False):
        if right:
            return (x < X - 1, lambda: w_copy(block, part, 2, {"ctx": me + 1}, own))
        return (x > 0, lambda: w_copy(block, part, 3, {"ctx": me - 1}, own))

    pending = []

    def issue(guard, entry):
        cond, make = entry
        if guard is not None:
            cond = jnp.logical_and(guard, cond)

        @pl.when(cond)
        def _():
            make().start()

        pending.append((cond, make))

    def cross(guard, block, part):
        if crossing:
            cond = part == 2 * q
            if guard is not None:
                cond = jnp.logical_and(guard, cond)
            make = lambda: w_copy(block, part, 4, {"dp": dp + 1 - 2 * q})

            @pl.when(cond)
            def _():
                make().start()

            pending.append((cond, make))

    def arrived(guard, block, part):
        @pl.when(guard)
        def _():
            w_copy(block, part, 0, {"ctx": me}).wait_recv()

    def start_weights():
        for j in range(parts):
            for entry in (
                sends_z(me, q + j, True, True),
                sends_z(me, q + j, False, True),
                sends_x(me, q + j, True, True),
                sends_x(me, q + j, False, True),
            ):
                issue(None, entry)

    def spread_x(step):
        for t in range(1, X):
            for j in range(parts):
                part = q + j
                for sign in (-1, 1):
                    for side in ((0,) if step == 0 else (-1, 1)):
                        zz = z + side * step
                        xx = x + sign * t
                        guard = functools.reduce(
                            jnp.logical_and, [zz >= 0, zz < Z, xx >= 0, xx < X]
                        )
                        block = jnp.clip(zz, 0, Z - 1) * X + jnp.clip(xx, 0, X - 1)
                        arrived(guard, block, part)
                        if t < X - 1:
                            issue(guard, sends_x(block, part, sign < 0))
                        cross(guard, block, part)

    def gather_weights():
        for step in range(1, Z):
            for j in range(parts):
                part = q + j
                for up in (True, False):
                    zz = z - step if up else z + step
                    guard = zz >= 0 if up else zz < Z
                    block = jnp.clip(zz, 0, Z - 1) * X + x
                    arrived(guard, block, part)
                    if step < Z - 1:
                        issue(guard, sends_z(block, part, up))
                    issue(guard, sends_x(block, part, True))
                    issue(guard, sends_x(block, part, False))
                    cross(guard, block, part)
            spread_x(step - 1)
        spread_x(Z - 1)
        if crossing:
            for k in range(1, n):
                block = lax.rem(me + k, n)
                w_copy(block, 2 - 2 * q, 4, {"dp": dp}).wait_recv()

    def halo_copies(which, src, dst):
        down = pltpu.make_async_remote_copy(
            src_ref=src.at[pl.ds(0, DMAX)], dst_ref=dst.at[pl.ds(DMAX, DMAX)],
            send_sem=h_send.at[which, 0], recv_sem=h_recv.at[which, 1],
            device_id={"ctx": me - 1}, device_id_type=MESH,
        )
        up = pltpu.make_async_remote_copy(
            src_ref=src.at[pl.ds(length - DMAX, DMAX)], dst_ref=dst.at[pl.ds(0, DMAX)],
            send_sem=h_send.at[which, 1], recv_sem=h_recv.at[which, 0],
            device_id={"ctx": me + 1}, device_id_type=MESH,
        )
        return down, up

    def start_halo(which, src, dst):
        down, up = halo_copies(which, src, dst)

        @pl.when(me > 0)
        def _():
            down.start()

        @pl.when(me == 0)
        def _():
            dst[pl.ds(0, DMAX), :] = jnp.zeros((DMAX, width), BF16)

        @pl.when(me < n - 1)
        def _():
            up.start()

        @pl.when(me == n - 1)
        def _():
            dst[pl.ds(DMAX, DMAX), :] = jnp.zeros((DMAX, width), BF16)

    def wait_halo(which, src, dst):
        down, up = halo_copies(which, src, dst)

        @pl.when(me > 0)
        def _():
            up.wait_recv()
            down.wait_send()

        @pl.when(me < n - 1)
        def _():
            down.wait_recv()
            up.wait_send()

    dilation = dil_ref[seg]
    tile = 256

    def selectors():
        t = lax.broadcasted_iota(jnp.int32, (length, length), 0)
        s = lax.broadcasted_iota(jnp.int32, (length, length), 1)
        th = lax.broadcasted_iota(jnp.int32, (length, 2 * DMAX), 0)
        h = lax.broadcasted_iota(jnp.int32, (length, 2 * DMAX), 1)
        one = lambda c: jnp.where(c, 1.0, 0.0).astype(BF16)
        before = (one(s == t - dilation), one((h - DMAX == th - dilation) & (h < DMAX)))
        after = (one(s == t + dilation), one((h - DMAX + length == th + dilation) & (h >= DMAX)))
        return before, after

    def convolve(src, halo, dst, flip):
        before, after = selectors()
        low, high = (2, 0) if flip else (0, 2)

        def body(c, carry):
            cols = pl.ds(pl.multiple_of(c * tile, tile), tile)
            own, edge = src[:, cols], halo[:, cols]
            pick = lambda sel: jnp.dot(sel[0], own, preferred_element_type=F32) + jnp.dot(
                sel[1], edge, preferred_element_type=F32
            )
            value = tap_ref[pl.ds(1, 1), cols] * own.astype(F32)
            value = tap_ref[pl.ds(low, 1), cols] * pick(before) + value
            value = value + tap_ref[pl.ds(high, 1), cols] * pick(after)
            dst[:, cols] = value.astype(dst.dtype)
            return carry

        lax.fori_loop(0, width // tile, body, 0)

    step_rows = 16

    def activate(src, dst):
        def body(i, carry):
            at = pl.ds(pl.multiple_of(i * step_rows, step_rows), step_rows)
            r = src[at, :].astype(F32)
            s = lax.rsqrt(jnp.mean(r * r, axis=-1, keepdims=True) + 1e-06)
            v = r * s
            t = jnp.tanh(ROOT * (v + CUBIC * (v * v * v)))
            dst[at, :] = (0.5 * v * (1.0 + t)).astype(BF16)
            return carry

        lax.fori_loop(0, length // step_rows, body, 0)

    def pull_back(src, grad, store):
        def body(i, carry):
            at = pl.ds(pl.multiple_of(i * step_rows, step_rows), step_rows)
            r = src[at, :].astype(F32)
            s = lax.rsqrt(jnp.mean(r * r, axis=-1, keepdims=True) + 1e-06)
            v = r * s
            vv = v * v
            t = jnp.tanh(ROOT * (v + CUBIC * (vv * v)))
            half = 0.5 * (1.0 + t)
            slope = half + 0.5 * v * (1.0 - t * t) * (ROOT * (1.0 + 3.0 * CUBIC * vv))
            dn = ga[at, :] * slope
            gr = s * (dn - v * jnp.mean(dn * v, axis=-1, keepdims=True))
            store(at, v * half, grad[at, :].astype(F32) + gr)
            return carry

        lax.fori_loop(0, length // step_rows, body, 0)

    def project(grad):
        pb[...] = jnp.dot(grad[...], proj_ref[...], preferred_element_type=F32).astype(BF16)

    def sketch():
        def body(c, carry):
            cols = pl.ds(pl.multiple_of(c * tile, tile), tile)
            value = lax.dot_general(
                pb[...], mixed[:, cols], (((0,), (0,)), ((), ())), preferred_element_type=F32
            ).astype(BF16)
            for k in range(n):
                sk[k, :, cols] = value[k * kr : (k + 1) * kr]
            return carry

        lax.fori_loop(0, width // tile, body, 0)
        for k in range(1, n):
            rs_copy(lax.rem(me + k, n)).start()

    def rs_copy(peer):
        return pltpu.make_async_remote_copy(
            src_ref=sk.at[peer], dst_ref=rs.at[me],
            send_sem=rs_send.at[peer], recv_sem=rs_recv.at[me],
            device_id={"ctx": peer}, device_id_type=MESH,
        )

    def back_product(grad):
        def body(c, carry):
            cols = pl.ds(pl.multiple_of(c * tile, tile), tile)
            gu[:, cols] = lax.dot_general(
                grad[...], wf[cols, :], (((1,), (1,)), ((), ())), preferred_element_type=F32
            ).astype(BF16)
            return carry

        lax.fori_loop(0, width // tile, body, 0)

    def core_copy(index, src, dst):
        return pltpu.make_async_remote_copy(
            src_ref=src, dst_ref=dst, send_sem=c_send.at[index], recv_sem=c_recv.at[index],
            device_id={"segment": 1 - seg}, device_id_type=MESH,
        )

    half = width // 2
    mid_copy = core_copy(0, first, second)
    back_copy = core_copy(1, first, second)
    half_copy = core_copy(2, other, out_ref)

    start_weights()
    wf[pl.ds(pl.multiple_of(me * rows, 16), rows), :] = w_ref[...]

    @pl.when(seg == 0)
    def _():
        activate(x_ref, act)
        start_halo(0, act, halo_a)

    @pl.when(seg == 1)
    def _():
        project(g_ref)

    gather_weights()

    @pl.when(seg == 0)
    def _():
        wait_halo(0, act, halo_a)
        convolve(act, halo_a, mixed, False)

        def body(c, carry):
            cols = pl.ds(pl.multiple_of(c * tile, tile), tile)
            value = jnp.dot(mixed[...], wf[:, cols], preferred_element_type=F32)
            first[:, cols] = (x_ref[:, cols].astype(F32) + value).astype(BF16)
            return carry

        lax.fori_loop(0, width // tile, body, 0)
        mid_copy.start()
        mid_copy.wait_send()
        back_copy.wait_recv()
        project(second)
        sketch()
        back_product(second)
        start_halo(1, gu, halo_g)
        wait_halo(1, gu, halo_g)
        convolve(gu, halo_g, ga, True)

        def store(at, value, grad):
            out_ref[at, :] = grad[:, :half].astype(BF16)
            other[at, :] = grad[:, half:].astype(BF16)

        pull_back(x_ref, second, store)
        half_copy.start()
        half_copy.wait_send()

    @pl.when(seg == 1)
    def _():
        back_product(g_ref)
        start_halo(1, gu, halo_g)
        wait_halo(1, gu, halo_g)
        convolve(gu, halo_g, ga, True)
        mid_copy.wait_recv()

        def store(at, value, grad):
            act[at, :] = value.astype(BF16)
            first[at, :] = grad.astype(BF16)

        pull_back(second, g_ref, store)
        back_copy.start()
        start_halo(0, act, halo_a)
        wait_halo(0, act, halo_a)
        convolve(act, halo_a, mixed, False)
        sketch()
        back_copy.wait_send()
        half_copy.wait_recv()

    total = sk[me].astype(F32)
    for k in range(1, n):
        peer = lax.rem(me + k, n)
        pltpu.make_async_remote_copy(
            src_ref=sk.at[peer], dst_ref=rs.at[peer], send_sem=rs_send.at[peer],
            recv_sem=rs_recv.at[peer], device_id={"ctx": peer}, device_id_type=MESH,
        ).wait_recv()
        total = total + rs[peer].astype(F32)
    dpb[dp] = total.astype(BF16)

    def dp_copy(peer, slot):
        return pltpu.make_async_remote_copy(
            src_ref=dpb.at[slot], dst_ref=dpb.at[slot], send_sem=dp_send.at[peer],
            recv_sem=dp_recv.at[slot], device_id={"dp": peer}, device_id_type=MESH,
        )

    for k in range(1, m):
        dp_copy(lax.rem(dp + k, m), dp).start()
    for k in range(1, m):
        dp_copy(lax.rem(dp + k, m), lax.rem(dp + k, m)).wait_recv()
    merged = dpb[0].astype(F32)
    for k in range(1, m):
        merged = merged + dpb[k].astype(F32)
    sk_ref[...] = merged

    for k in range(1, m):
        dp_copy(lax.rem(dp + k, m), dp).wait_send()
    for k in range(1, n):
        rs_copy(lax.rem(me + k, n)).wait_send()
    for cond, make in pending:

        @pl.when(cond)
        def _():
            make().wait_send()


def shards(inputs, cotangent, weights, tap_weights, projection, dilations):
    n, m = lax.axis_size("ctx"), lax.axis_size("dp")
    length, width = inputs.shape[1:]
    rows = weights.shape[1]
    tests = projection.shape[2]
    kr = tests // n
    vmem = pl.BlockSpec(memory_space=pltpu.VMEM)
    dma = pltpu.SemaphoreType.DMA
    grad, sketches = pl.pallas_call(
        functools.partial(kernel, n, m),
        out_shape=(
            jax.ShapeDtypeStruct((length, width // 2), BF16),
            jax.ShapeDtypeStruct((kr, width), F32),
        ),
        in_specs=[vmem] * 5 + [pl.BlockSpec(memory_space=pltpu.SMEM)],
        out_specs=(vmem, vmem),
        scratch_shapes=[
            pltpu.VMEM((n * rows, width), BF16),
            pltpu.VMEM((length, width), BF16),
            pltpu.VMEM((2 * DMAX, width), BF16),
            pltpu.VMEM((2 * DMAX, width), BF16),
            pltpu.VMEM((length, width), BF16),
            pltpu.VMEM((length, width), BF16),
            pltpu.VMEM((length, width), F32),
            pltpu.VMEM((length, width), BF16),
            pltpu.VMEM((length, width), BF16),
            pltpu.VMEM((length, width // 2), BF16),
            pltpu.VMEM((n, kr, width), BF16),
            pltpu.VMEM((n, kr, width), BF16),
            pltpu.VMEM((m, kr, width), BF16),
            pltpu.VMEM((length, tests), BF16),
            dma((n, 3, 5)),
            dma((n, 3)),
            dma((2, 2)),
            dma((2, 2)),
            dma((3,)),
            dma((3,)),
            dma((n,)),
            dma((n,)),
            dma((m,)),
            dma((m,)),
        ],
        compiler_params=pltpu.CompilerParams(
            collective_id=0, has_side_effects=True, vmem_limit_bytes=48 << 20
        ),
        name="segment",
    )(inputs[0], cotangent[0], weights[0], tap_weights[0], projection[0], dilations)
    return (grad[None], sketches[None])


def solution(mesh):
    in_specs = (
        P("dp", "ctx", None),
        P("dp", "ctx", None),
        P("segment", "ctx", None),
        P("segment", None, None),
        P("segment", None, None),
        P(),
    )
    out_specs = (P("dp", "ctx", "segment"), P("segment", "ctx", None))
    return jax.shard_map(shards, mesh=mesh, in_specs=in_specs, out_specs=out_specs, check_vma=False)
```

```python
import functools

import jax
import jax.numpy as jnp
from jax import lax
from jax.experimental import pallas as pl
from jax.experimental.pallas import tpu as pltpu
from jax.sharding import PartitionSpec as P

DMAX = 64
MESH = pl.DeviceIdType.MESH
F32 = jnp.float32
BF16 = jnp.bfloat16
ROOT = 0.7978845608028654
CUBIC = 0.044715


def line_width(n):
    width = 1
    while 4 * width * width <= n:
        width *= 2
    return width


def kernel(
    n, m, x_hbm, g_hbm, w_hbm, tap_hbm, proj_hbm, dil_hbm, out_ref, sk_ref,
    io_ref, tap_ref, proj_ref, dil_ref, slope, normed, scale, l_sem, wf, act, halo_a, halo_g, mixed, gu, ga, first, second, other, sk, rs, dpb, pb,
    w_send, w_recv, h_send, h_recv, c_send, c_recv, rs_send, rs_recv, dp_send, dp_recv,
):
    me = lax.axis_index("ctx")
    dp = lax.axis_index("dp")
    seg = lax.axis_index("segment")
    length, width = io_ref.shape
    rows = w_hbm.shape[1]
    w_ref = w_hbm.at[0]
    kr = sk.shape[1]
    X = line_width(n)
    Z = n // X
    z = me // X
    x = lax.rem(me, X)
    crossing = m % 2 == 0 and rows % 48 == 0
    parts = 2 if crossing else 1
    pr = rows // 3 if crossing else rows
    q = lax.rem(dp, 2) if crossing else 0

    own_rows = pl.ds(pl.multiple_of(me * rows, 16), rows)
    loads = [
        pltpu.make_async_copy(w_ref, wf.at[own_rows], l_sem.at[0]),
        pltpu.make_async_copy(proj_hbm.at[0], proj_ref, l_sem.at[1]),
        pltpu.make_async_copy(tap_hbm.at[0], tap_ref, l_sem.at[2]),
        pltpu.make_async_copy(dil_hbm, dil_ref, l_sem.at[3]),
    ]

    @pl.when(seg == 0)
    def _():
        pltpu.make_async_copy(x_hbm.at[0], io_ref, l_sem.at[4]).start()

    @pl.when(seg == 1)
    def _():
        pltpu.make_async_copy(g_hbm.at[0], io_ref, l_sem.at[4]).start()

    for load in loads:
        load.start()

    barrier = pltpu.get_barrier_semaphore()
    for k in range(1, n):
        pl.semaphore_signal(barrier, inc=1, device_id={"ctx": lax.rem(me + k, n)}, device_id_type=MESH)
    for k in range(1, m):
        pl.semaphore_signal(barrier, inc=1, device_id={"dp": lax.rem(dp + k, m)}, device_id_type=MESH)
    pl.semaphore_signal(barrier, inc=1, device_id={"segment": 1 - seg}, device_id_type=MESH)
    pl.semaphore_wait(barrier, n + m - 1)

    def piece(block, part):
        return pl.ds(pl.multiple_of(block * rows + part * pr, 16), pr)

    def w_copy(block, part, direction, where, own=False):
        src = w_ref.at[pl.ds(pl.multiple_of(part * pr, 16), pr)] if own else wf.at[piece(block, part)]
        return pltpu.make_async_remote_copy(
            src_ref=src,
            dst_ref=wf.at[piece(block, part)],
            send_sem=w_send.at[block, part, direction],
            recv_sem=w_recv.at[block, part],
            device_id=where,
            device_id_type=MESH,
        )

    def sends_z(block, part, up, own=False):
        if up:
            return (z < Z - 1, lambda: w_copy(block, part, 0, {"ctx": me + X}, own))
        return (z > 0, lambda: w_copy(block, part, 1, {"ctx": me - X}, own))

    def sends_x(block, part, right, own=False):
        if right:
            return (x < X - 1, lambda: w_copy(block, part, 2, {"ctx": me + 1}, own))
        return (x > 0, lambda: w_copy(block, part, 3, {"ctx": me - 1}, own))

    pending = []

    def issue(guard, entry):
        cond, make = entry
        if guard is not None:
            cond = jnp.logical_and(guard, cond)

        @pl.when(cond)
        def _():
            make().start()

        pending.append((cond, make))

    def cross(guard, block, part):
        if crossing:
            cond = part == 2 * q
            if guard is not None:
                cond = jnp.logical_and(guard, cond)
            make = lambda: w_copy(block, part, 4, {"dp": dp + 1 - 2 * q})

            @pl.when(cond)
            def _():
                make().start()

            pending.append((cond, make))

    def arrived(guard, block, part):
        @pl.when(guard)
        def _():
            w_copy(block, part, 0, {"ctx": me}).wait_recv()

    def start_weights():
        for j in range(parts):
            for entry in (
                sends_z(me, q + j, True, True),
                sends_z(me, q + j, False, True),
                sends_x(me, q + j, True, True),
                sends_x(me, q + j, False, True),
            ):
                issue(None, entry)

    def spread_x(step):
        for t in range(1, X):
            for j in range(parts):
                part = q + j
                for sign in (-1, 1):
                    for side in ((0,) if step == 0 else (-1, 1)):
                        zz = z + side * step
                        xx = x + sign * t
                        guard = functools.reduce(
                            jnp.logical_and, [zz >= 0, zz < Z, xx >= 0, xx < X]
                        )
                        block = jnp.clip(zz, 0, Z - 1) * X + jnp.clip(xx, 0, X - 1)
                        arrived(guard, block, part)
                        if t < X - 1:
                            issue(guard, sends_x(block, part, sign < 0))
                        cross(guard, block, part)

    def gather_weights():
        for step in range(1, Z):
            for j in range(parts):
                part = q + j
                for up in (True, False):
                    zz = z - step if up else z + step
                    guard = zz >= 0 if up else zz < Z
                    block = jnp.clip(zz, 0, Z - 1) * X + x
                    arrived(guard, block, part)
                    if step < Z - 1:
                        issue(guard, sends_z(block, part, up))
                    issue(guard, sends_x(block, part, True))
                    issue(guard, sends_x(block, part, False))
                    cross(guard, block, part)
            spread_x(step - 1)
        spread_x(Z - 1)
        if crossing:
            for k in range(1, n):
                block = lax.rem(me + k, n)
                w_copy(block, 2 - 2 * q, 4, {"dp": dp}).wait_recv()

    def halo_copies(which, src, dst):
        down = pltpu.make_async_remote_copy(
            src_ref=src.at[pl.ds(0, DMAX)], dst_ref=dst.at[pl.ds(DMAX, DMAX)],
            send_sem=h_send.at[which, 0], recv_sem=h_recv.at[which, 1],
            device_id={"ctx": me - 1}, device_id_type=MESH,
        )
        up = pltpu.make_async_remote_copy(
            src_ref=src.at[pl.ds(length - DMAX, DMAX)], dst_ref=dst.at[pl.ds(0, DMAX)],
            send_sem=h_send.at[which, 1], recv_sem=h_recv.at[which, 0],
            device_id={"ctx": me + 1}, device_id_type=MESH,
        )
        return down, up

    def start_halo(which, src, dst):
        down, up = halo_copies(which, src, dst)

        @pl.when(me > 0)
        def _():
            down.start()

        @pl.when(me == 0)
        def _():
            dst[pl.ds(0, DMAX), :] = jnp.zeros((DMAX, width), BF16)

        @pl.when(me < n - 1)
        def _():
            up.start()

        @pl.when(me == n - 1)
        def _():
            dst[pl.ds(DMAX, DMAX), :] = jnp.zeros((DMAX, width), BF16)

    def wait_halo(which, src, dst):
        down, up = halo_copies(which, src, dst)

        @pl.when(me > 0)
        def _():
            up.wait_recv()
            down.wait_send()

        @pl.when(me < n - 1)
        def _():
            down.wait_recv()
            up.wait_send()

    tile = 256

    def selectors():
        dilation = dil_ref[seg]
        t = lax.broadcasted_iota(jnp.int32, (length, length), 0)
        s = lax.broadcasted_iota(jnp.int32, (length, length), 1)
        th = lax.broadcasted_iota(jnp.int32, (length, 2 * DMAX), 0)
        h = lax.broadcasted_iota(jnp.int32, (length, 2 * DMAX), 1)
        one = lambda c: jnp.where(c, 1.0, 0.0).astype(BF16)
        before = (one(s == t - dilation), one((h - DMAX == th - dilation) & (h < DMAX)))
        after = (one(s == t + dilation), one((h - DMAX + length == th + dilation) & (h >= DMAX)))
        return before, after

    def convolve(src, halo, dst, flip):
        before, after = selectors()
        low, high = (2, 0) if flip else (0, 2)

        def body(c, carry):
            cols = pl.ds(pl.multiple_of(c * tile, tile), tile)
            own, edge = src[:, cols], halo[:, cols]
            pick = lambda sel: jnp.dot(sel[0], own, preferred_element_type=F32) + jnp.dot(
                sel[1], edge, preferred_element_type=F32
            )
            value = tap_ref[pl.ds(1, 1), cols] * own.astype(F32)
            value = tap_ref[pl.ds(low, 1), cols] * pick(before) + value
            value = value + tap_ref[pl.ds(high, 1), cols] * pick(after)
            dst[:, cols] = value.astype(dst.dtype)
            return carry

        lax.fori_loop(0, width // tile, body, 0)

    step_rows = 16

    def prepare(src):
        def body(i, carry):
            at = pl.ds(pl.multiple_of(i * step_rows, step_rows), step_rows)
            r = src[at, :].astype(F32)
            s = lax.rsqrt(jnp.mean(r * r, axis=-1, keepdims=True) + 1e-06)
            v = r * s
            vv = v * v
            t = jnp.tanh(ROOT * (v + CUBIC * (vv * v)))
            half = 0.5 * (1.0 + t)
            act[at, :] = (v * half).astype(BF16)
            slope[at, :] = half + 0.5 * v * (1.0 - t * t) * (ROOT * (1.0 + 3.0 * CUBIC * vv))
            normed[at, :] = v
            scale[at, :] = jnp.broadcast_to(s, (step_rows, 128))
            return carry

        lax.fori_loop(0, length // step_rows, body, 0)

    chunk = 64

    def pull_back(grad, store, send):
        def outer(c, carry):
            def body(i, carry):
                at = pl.ds(pl.multiple_of(c * chunk + i * step_rows, step_rows), step_rows)
                v = normed[at, :]
                s = scale[at, :][:, :1]
                dn = ga[at, :] * slope[at, :]
                gr = s * (dn - v * jnp.mean(dn * v, axis=-1, keepdims=True))
                store(at, grad[at, :].astype(F32) + gr)
                return carry

            lax.fori_loop(0, chunk // step_rows, body, 0)
            send(c).start()
            return carry

        lax.fori_loop(0, length // chunk, outer, 0)

    def project(grad):
        pb[...] = jnp.dot(grad[...], proj_ref[...], preferred_element_type=F32).astype(BF16)

    def sketch():
        def body(c, carry):
            cols = pl.ds(pl.multiple_of(c * tile, tile), tile)
            value = lax.dot_general(
                pb[...], mixed[:, cols], (((0,), (0,)), ((), ())), preferred_element_type=F32
            ).astype(BF16)
            for k in range(n):
                sk[k, :, cols] = value[k * kr : (k + 1) * kr]
            return carry

        lax.fori_loop(0, width // tile, body, 0)
        for k in range(1, n):
            rs_copy(lax.rem(me + k, n)).start()

    def rs_copy(peer):
        return pltpu.make_async_remote_copy(
            src_ref=sk.at[peer], dst_ref=rs.at[me],
            send_sem=rs_send.at[peer], recv_sem=rs_recv.at[me],
            device_id={"ctx": peer}, device_id_type=MESH,
        )

    def back_product(grad):
        def body(c, carry):
            cols = pl.ds(pl.multiple_of(c * tile, tile), tile)
            gu[:, cols] = lax.dot_general(
                grad[...], wf[cols, :], (((1,), (1,)), ((), ())), preferred_element_type=F32
            ).astype(BF16)
            return carry

        lax.fori_loop(0, width // tile, body, 0)

    def core_copy(index, src, dst):
        return pltpu.make_async_remote_copy(
            src_ref=src, dst_ref=dst, send_sem=c_send.at[index], recv_sem=c_recv.at[index],
            device_id={"segment": 1 - seg}, device_id_type=MESH,
        )

    half = width // 2
    tiles, chunks = width // tile, length // chunk

    def mid_copy(c):
        cols = pl.ds(pl.multiple_of(c * tile, tile), tile)
        return core_copy(c, first.at[:, cols], second.at[:, cols])

    def back_copy(c):
        at = pl.ds(pl.multiple_of(c * chunk, chunk), chunk)
        return core_copy(tiles + c, first.at[at], second.at[at])

    def half_copy(c):
        at = pl.ds(pl.multiple_of(c * chunk, chunk), chunk)
        return core_copy(tiles + chunks + c, other.at[at], out_ref.at[at])

    start_weights()
    pltpu.make_async_copy(x_hbm.at[0], io_ref, l_sem.at[4]).wait()
    for load in loads:
        load.wait()

    @pl.when(seg == 0)
    def _():
        prepare(io_ref)
        start_halo(0, act, halo_a)

    @pl.when(seg == 1)
    def _():
        project(io_ref)

    gather_weights()

    @pl.when(seg == 0)
    def _():
        wait_halo(0, act, halo_a)
        convolve(act, halo_a, mixed, False)

        def body(c, carry):
            cols = pl.ds(pl.multiple_of(c * tile, tile), tile)
            value = jnp.dot(mixed[...], wf[:, cols], preferred_element_type=F32)
            first[:, cols] = (io_ref[:, cols].astype(F32) + value).astype(BF16)
            mid_copy(c).start()
            return carry

        lax.fori_loop(0, tiles, body, 0)
        for c in range(tiles):
            mid_copy(c).wait_send()
        for c in range(chunks):
            back_copy(c).wait_recv()
        project(second)
        sketch()
        back_product(second)
        start_halo(1, gu, halo_g)
        wait_halo(1, gu, halo_g)
        convolve(gu, halo_g, ga, True)

        def store(at, grad):
            out_ref[at, :] = grad[:, :half].astype(BF16)
            other[at, :] = grad[:, half:].astype(BF16)

        pull_back(second, store, half_copy)
        for c in range(chunks):
            half_copy(c).wait_send()

    @pl.when(seg == 1)
    def _():
        back_product(io_ref)
        start_halo(1, gu, halo_g)
        for c in range(tiles):
            mid_copy(c).wait_recv()
        prepare(second)
        start_halo(0, act, halo_a)
        wait_halo(1, gu, halo_g)
        convolve(gu, halo_g, ga, True)

        def store(at, grad):
            first[at, :] = grad.astype(BF16)

        pull_back(io_ref, store, back_copy)
        wait_halo(0, act, halo_a)
        convolve(act, halo_a, mixed, False)
        sketch()
        for c in range(chunks):
            back_copy(c).wait_send()
        for c in range(chunks):
            half_copy(c).wait_recv()

    total = sk[me].astype(F32)
    for k in range(1, n):
        peer = lax.rem(me + k, n)
        pltpu.make_async_remote_copy(
            src_ref=sk.at[peer], dst_ref=rs.at[peer], send_sem=rs_send.at[peer],
            recv_sem=rs_recv.at[peer], device_id={"ctx": peer}, device_id_type=MESH,
        ).wait_recv()
        total = total + rs[peer].astype(F32)
    dpb[dp] = total.astype(BF16)

    def dp_copy(peer, slot):
        return pltpu.make_async_remote_copy(
            src_ref=dpb.at[slot], dst_ref=dpb.at[slot], send_sem=dp_send.at[peer],
            recv_sem=dp_recv.at[slot], device_id={"dp": peer}, device_id_type=MESH,
        )

    for k in range(1, m):
        dp_copy(lax.rem(dp + k, m), dp).start()
    for k in range(1, m):
        dp_copy(lax.rem(dp + k, m), lax.rem(dp + k, m)).wait_recv()
    merged = dpb[0].astype(F32)
    for k in range(1, m):
        merged = merged + dpb[k].astype(F32)
    sk_ref[...] = merged

    for k in range(1, m):
        dp_copy(lax.rem(dp + k, m), dp).wait_send()
    for k in range(1, n):
        rs_copy(lax.rem(me + k, n)).wait_send()
    for cond, make in pending:

        @pl.when(cond)
        def _():
            make().wait_send()


def shards(inputs, cotangent, weights, tap_weights, projection, dilations):
    n, m = lax.axis_size("ctx"), lax.axis_size("dp")
    length, width = inputs.shape[1:]
    rows = weights.shape[1]
    tests = projection.shape[2]
    kr = tests // n
    vmem = pl.BlockSpec(memory_space=pltpu.VMEM)
    dma = pltpu.SemaphoreType.DMA
    grad, sketches = pl.pallas_call(
        functools.partial(kernel, n, m),
        out_shape=(
            jax.ShapeDtypeStruct((length, width // 2), BF16),
            jax.ShapeDtypeStruct((kr, width), F32),
        ),
        in_specs=[pl.BlockSpec(memory_space=pl.ANY)] * 6,
        out_specs=(vmem, vmem),
        scratch_shapes=[
            pltpu.VMEM((length, width), BF16),
            pltpu.VMEM(tap_weights.shape[1:], F32),
            pltpu.VMEM(projection.shape[1:], BF16),
            pltpu.SMEM(dilations.shape, jnp.int32),
            pltpu.VMEM((length, width), F32),
            pltpu.VMEM((length, width), F32),
            pltpu.VMEM((length, 128), F32),
            dma((5,)),
            pltpu.VMEM((n * rows, width), BF16),
            pltpu.VMEM((length, width), BF16),
            pltpu.VMEM((2 * DMAX, width), BF16),
            pltpu.VMEM((2 * DMAX, width), BF16),
            pltpu.VMEM((length, width), BF16),
            pltpu.VMEM((length, width), BF16),
            pltpu.VMEM((length, width), F32),
            pltpu.VMEM((length, width), BF16),
            pltpu.VMEM((length, width), BF16),
            pltpu.VMEM((length, width // 2), BF16),
            pltpu.VMEM((n, kr, width), BF16),
            pltpu.VMEM((n, kr, width), BF16),
            pltpu.VMEM((m, kr, width), BF16),
            pltpu.VMEM((length, tests), BF16),
            dma((n, 3, 5)),
            dma((n, 3)),
            dma((2, 2)),
            dma((2, 2)),
            dma((width // 256 + 2 * length // 64,)),
            dma((width // 256 + 2 * length // 64,)),
            dma((n,)),
            dma((n,)),
            dma((m,)),
            dma((m,)),
        ],
        compiler_params=pltpu.CompilerParams(
            collective_id=0, has_side_effects=True, vmem_limit_bytes=60 << 20
        ),
        name="segment",
    )(inputs, cotangent, weights, tap_weights, projection, dilations)
    return (grad[None], sketches[None])


def solution(mesh):
    in_specs = (
        P("dp", "ctx", None),
        P("dp", "ctx", None),
        P("segment", "ctx", None),
        P("segment", None, None),
        P("segment", None, None),
        P(),
    )
    out_specs = (P("dp", "ctx", "segment"), P("segment", "ctx", None))
    return jax.shard_map(shards, mesh=mesh, in_specs=in_specs, out_specs=out_specs, check_vma=False)
```

```python
import functools

import jax
import jax.numpy as jnp
from jax import lax
from jax.experimental import pallas as pl
from jax.experimental.pallas import tpu as pltpu
from jax.sharding import PartitionSpec as P

DMAX = 64
MESH = pl.DeviceIdType.MESH
F32 = jnp.float32
BF16 = jnp.bfloat16
ROOT = 0.7978845608028654
CUBIC = 0.044715


def line_width(n):
    width = 1
    while 4 * width * width <= n:
        width *= 2
    return width


def kernel(
    n, m, x_hbm, g_hbm, w_hbm, tap_ref, proj_hbm, dil_hbm, out_ref, sk_ref,
    io_ref, proj_ref, dil_ref, slope, normed, scale, l_sem, wf, act, halo_a, halo_g, mixed, gu, ga, first, second, other, sk, rs, dpb, pb, ys, yr, keep,
    w_send, w_recv, h_send, h_recv, c_send, c_recv, rs_send, rs_recv, dp_send, dp_recv,
    y_send, y_recv,
):
    me = lax.axis_index("ctx")
    dp = lax.axis_index("dp")
    seg = lax.axis_index("segment")
    length, width = io_ref.shape
    rows = w_hbm.shape[1]
    w_ref = w_hbm.at[0]
    kr = sk.shape[-2]
    X = line_width(n)
    Z = n // X
    z = me // X
    x = lax.rem(me, X)
    crossing = m % 2 == 0 and rows % 48 == 0
    parts = 2 if crossing else 1
    pr = rows // 3 if crossing else rows
    q = lax.rem(dp, 2) if crossing else 0

    own_rows = pl.ds(pl.multiple_of(me * rows, 16), rows)
    loads = [
        pltpu.make_async_copy(w_ref, wf.at[own_rows], l_sem.at[0]),
        pltpu.make_async_copy(proj_hbm.at[0], proj_ref, l_sem.at[1]),
        pltpu.make_async_copy(dil_hbm, dil_ref, l_sem.at[3]),
    ]

    @pl.when(seg == 0)
    def _():
        pltpu.make_async_copy(x_hbm.at[0], io_ref, l_sem.at[4]).start()

    @pl.when(seg == 1)
    def _():
        pltpu.make_async_copy(g_hbm.at[0], io_ref, l_sem.at[4]).start()

    for load in loads:
        load.start()

    barrier = pltpu.get_barrier_semaphore()
    for k in range(1, n):
        pl.semaphore_signal(barrier, inc=1, device_id={"ctx": lax.rem(me + k, n)}, device_id_type=MESH)
    for k in range(1, m):
        pl.semaphore_signal(barrier, inc=1, device_id={"dp": lax.rem(dp + k, m)}, device_id_type=MESH)
    pl.semaphore_signal(barrier, inc=1, device_id={"segment": 1 - seg}, device_id_type=MESH)
    pl.semaphore_wait(barrier, n + m - 1)

    def piece(block, part):
        return pl.ds(pl.multiple_of(block * rows + part * pr, 16), pr)

    def w_copy(block, part, direction, where, own=False):
        src = w_ref.at[pl.ds(pl.multiple_of(part * pr, 16), pr)] if own else wf.at[piece(block, part)]
        return pltpu.make_async_remote_copy(
            src_ref=src,
            dst_ref=wf.at[piece(block, part)],
            send_sem=w_send.at[block, part, direction],
            recv_sem=w_recv.at[block, part],
            device_id=where,
            device_id_type=MESH,
        )

    def sends_z(block, part, up, own=False):
        if up:
            return (z < Z - 1, lambda: w_copy(block, part, 0, {"ctx": me + X}, own))
        return (z > 0, lambda: w_copy(block, part, 1, {"ctx": me - X}, own))

    def sends_x(block, part, right, own=False):
        if right:
            return (x < X - 1, lambda: w_copy(block, part, 2, {"ctx": me + 1}, own))
        return (x > 0, lambda: w_copy(block, part, 3, {"ctx": me - 1}, own))

    pending = []

    def issue(guard, entry):
        cond, make = entry
        if guard is not None:
            cond = jnp.logical_and(guard, cond)

        @pl.when(cond)
        def _():
            make().start()

        pending.append((cond, make))

    def cross(guard, block, part):
        if crossing:
            cond = part == 2 * q
            if guard is not None:
                cond = jnp.logical_and(guard, cond)
            make = lambda: w_copy(block, part, 4, {"dp": dp + 1 - 2 * q})

            @pl.when(cond)
            def _():
                make().start()

            pending.append((cond, make))

    def arrived(guard, block, part):
        @pl.when(guard)
        def _():
            w_copy(block, part, 0, {"ctx": me}).wait_recv()

    def start_weights():
        for j in range(parts):
            for entry in (
                sends_z(me, q + j, True, True),
                sends_z(me, q + j, False, True),
                sends_x(me, q + j, True, True),
                sends_x(me, q + j, False, True),
            ):
                issue(None, entry)

    def spread_x(step):
        for t in range(1, X):
            for j in range(parts):
                part = q + j
                for sign in (-1, 1):
                    for side in ((0,) if step == 0 else (-1, 1)):
                        zz = z + side * step
                        xx = x + sign * t
                        guard = functools.reduce(
                            jnp.logical_and, [zz >= 0, zz < Z, xx >= 0, xx < X]
                        )
                        block = jnp.clip(zz, 0, Z - 1) * X + jnp.clip(xx, 0, X - 1)
                        arrived(guard, block, part)
                        if t < X - 1:
                            issue(guard, sends_x(block, part, sign < 0))
                        cross(guard, block, part)

    def gather_weights():
        for step in range(1, Z):
            for j in range(parts):
                part = q + j
                for up in (True, False):
                    zz = z - step if up else z + step
                    guard = zz >= 0 if up else zz < Z
                    block = jnp.clip(zz, 0, Z - 1) * X + x
                    arrived(guard, block, part)
                    if step < Z - 1:
                        issue(guard, sends_z(block, part, up))
                    issue(guard, sends_x(block, part, True))
                    issue(guard, sends_x(block, part, False))
                    cross(guard, block, part)
            spread_x(step - 1)
        spread_x(Z - 1)
        if crossing:
            for k in range(1, n):
                block = lax.rem(me + k, n)
                w_copy(block, 2 - 2 * q, 4, {"dp": dp}).wait_recv()

    def halo_copies(which, src, dst):
        down = pltpu.make_async_remote_copy(
            src_ref=src.at[pl.ds(0, DMAX)], dst_ref=dst.at[pl.ds(DMAX, DMAX)],
            send_sem=h_send.at[which, 0], recv_sem=h_recv.at[which, 1],
            device_id={"ctx": me - 1}, device_id_type=MESH,
        )
        up = pltpu.make_async_remote_copy(
            src_ref=src.at[pl.ds(length - DMAX, DMAX)], dst_ref=dst.at[pl.ds(0, DMAX)],
            send_sem=h_send.at[which, 1], recv_sem=h_recv.at[which, 0],
            device_id={"ctx": me + 1}, device_id_type=MESH,
        )
        return down, up

    def start_halo(which, src, dst):
        down, up = halo_copies(which, src, dst)

        @pl.when(me > 0)
        def _():
            down.start()

        @pl.when(me == 0)
        def _():
            dst[pl.ds(0, DMAX), :] = jnp.zeros((DMAX, width), BF16)

        @pl.when(me < n - 1)
        def _():
            up.start()

        @pl.when(me == n - 1)
        def _():
            dst[pl.ds(DMAX, DMAX), :] = jnp.zeros((DMAX, width), BF16)

    def wait_halo(which, src, dst):
        down, up = halo_copies(which, src, dst)

        @pl.when(me > 0)
        def _():
            up.wait_recv()
            down.wait_send()

        @pl.when(me < n - 1)
        def _():
            down.wait_recv()
            up.wait_send()

    paired = len(sk.shape) == 4

    tile = 256

    def selectors():
        dilation = dil_ref[seg]
        t = lax.broadcasted_iota(jnp.int32, (length, length), 0)
        s = lax.broadcasted_iota(jnp.int32, (length, length), 1)
        th = lax.broadcasted_iota(jnp.int32, (length, 2 * DMAX), 0)
        h = lax.broadcasted_iota(jnp.int32, (length, 2 * DMAX), 1)
        one = lambda c: jnp.where(c, 1.0, 0.0).astype(BF16)
        before = (one(s == t - dilation), one((h - DMAX == th - dilation) & (h < DMAX)))
        after = (one(s == t + dilation), one((h - DMAX + length == th + dilation) & (h >= DMAX)))
        return before, after

    def convolve(src, halo, dst, flip):
        before, after = selectors()
        low, high = (2, 0) if flip else (0, 2)

        def body(c, carry):
            cols = pl.ds(pl.multiple_of(c * tile, tile), tile)
            own, edge = src[:, cols], halo[:, cols]
            pick = lambda sel: jnp.dot(sel[0], own, preferred_element_type=F32) + jnp.dot(
                sel[1], edge, preferred_element_type=F32
            )
            value = tap_ref[pl.ds(1, 1), cols] * own.astype(F32)
            value = tap_ref[pl.ds(low, 1), cols] * pick(before) + value
            value = value + tap_ref[pl.ds(high, 1), cols] * pick(after)
            dst[:, cols] = value.astype(dst.dtype)
            return carry

        lax.fori_loop(0, width // tile, body, 0)

    step_rows = 16

    def prepare(src):
        def body(i, carry):
            at = pl.ds(pl.multiple_of(i * step_rows, step_rows), step_rows)
            r = src[at, :].astype(F32)
            s = lax.rsqrt(jnp.mean(r * r, axis=-1, keepdims=True) + 1e-06)
            v = r * s
            vv = v * v
            t = jnp.tanh(ROOT * (v + CUBIC * (vv * v)))
            half = 0.5 * (1.0 + t)
            act[at, :] = (v * half).astype(BF16)
            slope[at, :] = half + 0.5 * v * (1.0 - t * t) * (ROOT * (1.0 + 3.0 * CUBIC * vv))
            normed[at, :] = v
            scale[at, :] = jnp.broadcast_to(s, (step_rows, 128))
            return carry

        lax.fori_loop(0, length // step_rows, body, 0)

    chunk = 64

    def pull_back(grad, store, send):
        def outer(c, carry):
            def body(i, carry):
                at = pl.ds(pl.multiple_of(c * chunk + i * step_rows, step_rows), step_rows)
                v = normed[at, :]
                s = scale[at, :][:, :1]
                dn = ga[at, :] * slope[at, :]
                gr = s * (dn - v * jnp.mean(dn * v, axis=-1, keepdims=True))
                store(at, grad[at, :].astype(F32) + gr)
                return carry

            lax.fori_loop(0, chunk // step_rows, body, 0)
            send(c).start()
            return carry

        lax.fori_loop(0, length // chunk, outer, 0)

    def project(grad):
        pb[...] = jnp.dot(grad[...], proj_ref[...], preferred_element_type=F32).astype(BF16)

    pairs = ys.shape[0]

    def y_copy(k):
        return pltpu.make_async_remote_copy(
            src_ref=ys.at[k], dst_ref=yr.at[k], send_sem=y_send.at[k], recv_sem=y_recv.at[k],
            device_id={"dp": 1 - dp}, device_id_type=MESH,
        )

    def sketch_tile(c):
        cols = pl.ds(pl.multiple_of(c * tile, tile), tile)
        return lax.dot_general(
            pb[...], mixed[:, cols], (((0,), (0,)), ((), ())), preferred_element_type=F32
        )

    def sketch_pairs():
        def body(k, carry):
            value = sketch_tile(2 * k + 1 - dp).astype(BF16)
            for b in range(n):
                ys[k, b] = value[b * kr : (b + 1) * kr]
            y_copy(k).start()
            return carry

        lax.fori_loop(0, pairs, body, 0)

        def mine(k, carry):
            value = sketch_tile(2 * k + dp)
            for b in range(n):
                keep[k, b] = value[b * kr : (b + 1) * kr]
            return carry

        lax.fori_loop(0, pairs, mine, 0)

    def c_copy(k, peer, slot):
        return pltpu.make_async_remote_copy(
            src_ref=sk.at[k, peer], dst_ref=rs.at[k, slot], send_sem=rs_send.at[k, peer],
            recv_sem=rs_recv.at[k, slot], device_id={"ctx": peer}, device_id_type=MESH,
        )

    def spread_pairs():
        def body(k, carry):
            y_copy(k).wait_recv()
            sk[k] = (keep[k] + yr[k].astype(F32)).astype(BF16)
            for j in range(1, n):
                c_copy(k, lax.rem(me + j, n), me).start()
            return carry

        lax.fori_loop(0, pairs, body, 0)

    def d_copy(k, slot):
        return pltpu.make_async_remote_copy(
            src_ref=dpb.at[slot, k], dst_ref=dpb.at[slot, k], send_sem=dp_send.at[k],
            recv_sem=dp_recv.at[k], device_id={"dp": 1 - dp}, device_id_type=MESH,
        )

    def finish_pairs():
        def body(k, carry):
            total = sk[k, me].astype(F32)
            for j in range(1, n):
                peer = lax.rem(me + j, n)
                c_copy(k, peer, peer).wait_recv()
                total = total + rs[k, peer].astype(F32)
            dpb[dp, k] = total.astype(BF16)
            d_copy(k, dp).start()
            return carry

        lax.fori_loop(0, pairs, body, 0)
        for k in range(pairs):
            d_copy(k, 1 - dp).wait_recv()
            for slot in range(2):
                c = 2 * k + slot
                sk_ref[:, c * tile : (c + 1) * tile] = dpb[slot, k].astype(F32)
        for k in range(pairs):
            d_copy(k, dp).wait_send()
            y_copy(k).wait_send()
            for j in range(1, n):
                c_copy(k, lax.rem(me + j, n), me).wait_send()

    def sketch():
        if paired:
            return sketch_pairs()
        def body(c, carry):
            cols = pl.ds(pl.multiple_of(c * tile, tile), tile)
            value = lax.dot_general(
                pb[...], mixed[:, cols], (((0,), (0,)), ((), ())), preferred_element_type=F32
            ).astype(BF16)
            for k in range(n):
                sk[k, :, cols] = value[k * kr : (k + 1) * kr]
            return carry

        lax.fori_loop(0, width // tile, body, 0)
        for k in range(1, n):
            rs_copy(lax.rem(me + k, n)).start()

    def rs_copy(peer):
        return pltpu.make_async_remote_copy(
            src_ref=sk.at[peer], dst_ref=rs.at[me],
            send_sem=rs_send.at[peer], recv_sem=rs_recv.at[me],
            device_id={"ctx": peer}, device_id_type=MESH,
        )

    def back_product(grad):
        def body(c, carry):
            cols = pl.ds(pl.multiple_of(c * tile, tile), tile)
            gu[:, cols] = lax.dot_general(
                grad[...], wf[cols, :], (((1,), (1,)), ((), ())), preferred_element_type=F32
            ).astype(BF16)
            return carry

        lax.fori_loop(0, width // tile, body, 0)

    def core_copy(index, src, dst):
        return pltpu.make_async_remote_copy(
            src_ref=src, dst_ref=dst, send_sem=c_send.at[index], recv_sem=c_recv.at[index],
            device_id={"segment": 1 - seg}, device_id_type=MESH,
        )

    half = width // 2
    tiles, chunks = width // tile, length // chunk

    def mid_copy(c):
        cols = pl.ds(pl.multiple_of(c * tile, tile), tile)
        return core_copy(c, first.at[:, cols], second.at[:, cols])

    def back_copy(c):
        at = pl.ds(pl.multiple_of(c * chunk, chunk), chunk)
        return core_copy(tiles + c, first.at[at], second.at[at])

    def half_copy(c):
        at = pl.ds(pl.multiple_of(c * chunk, chunk), chunk)
        return core_copy(tiles + chunks + c, other.at[at], out_ref.at[at])

    start_weights()
    pltpu.make_async_copy(x_hbm.at[0], io_ref, l_sem.at[4]).wait()
    for load in loads:
        load.wait()

    @pl.when(seg == 0)
    def _():
        prepare(io_ref)
        start_halo(0, act, halo_a)

    @pl.when(seg == 1)
    def _():
        project(io_ref)

    gather_weights()

    @pl.when(seg == 0)
    def _():
        wait_halo(0, act, halo_a)
        convolve(act, halo_a, mixed, False)

        def body(c, carry):
            cols = pl.ds(pl.multiple_of(c * tile, tile), tile)
            value = jnp.dot(mixed[...], wf[:, cols], preferred_element_type=F32)
            first[:, cols] = (io_ref[:, cols].astype(F32) + value).astype(BF16)
            mid_copy(c).start()
            return carry

        lax.fori_loop(0, tiles, body, 0)
        for c in range(tiles):
            mid_copy(c).wait_send()
        for c in range(chunks):
            back_copy(c).wait_recv()
        project(second)
        sketch()
        back_product(second)
        start_halo(1, gu, halo_g)
        if paired:
            spread_pairs()
        wait_halo(1, gu, halo_g)
        convolve(gu, halo_g, ga, True)

        def store(at, grad):
            out_ref[at, :] = grad[:, :half].astype(BF16)
            other[at, :] = grad[:, half:].astype(BF16)

        pull_back(second, store, half_copy)
        for c in range(chunks):
            half_copy(c).wait_send()

    @pl.when(seg == 1)
    def _():
        back_product(io_ref)
        start_halo(1, gu, halo_g)
        for c in range(tiles):
            mid_copy(c).wait_recv()
        prepare(second)
        start_halo(0, act, halo_a)
        wait_halo(1, gu, halo_g)
        convolve(gu, halo_g, ga, True)

        def store(at, grad):
            first[at, :] = grad.astype(BF16)

        pull_back(io_ref, store, back_copy)
        wait_halo(0, act, halo_a)
        convolve(act, halo_a, mixed, False)
        sketch()
        if paired:
            spread_pairs()
        for c in range(chunks):
            back_copy(c).wait_send()
        for c in range(chunks):
            half_copy(c).wait_recv()

    def finish_direct():
        total = sk[me].astype(F32)
        for k in range(1, n):
            peer = lax.rem(me + k, n)
            pltpu.make_async_remote_copy(
                src_ref=sk.at[peer], dst_ref=rs.at[peer], send_sem=rs_send.at[peer],
                recv_sem=rs_recv.at[peer], device_id={"ctx": peer}, device_id_type=MESH,
            ).wait_recv()
            total = total + rs[peer].astype(F32)
        dpb[dp] = total.astype(BF16)

        def dp_copy(peer, slot):
            return pltpu.make_async_remote_copy(
                src_ref=dpb.at[slot], dst_ref=dpb.at[slot], send_sem=dp_send.at[peer],
                recv_sem=dp_recv.at[slot], device_id={"dp": peer}, device_id_type=MESH,
            )

        for k in range(1, m):
            dp_copy(lax.rem(dp + k, m), dp).start()
        for k in range(1, m):
            dp_copy(lax.rem(dp + k, m), lax.rem(dp + k, m)).wait_recv()
        merged = dpb[0].astype(F32)
        for k in range(1, m):
            merged = merged + dpb[k].astype(F32)
        sk_ref[...] = merged

        for k in range(1, m):
            dp_copy(lax.rem(dp + k, m), dp).wait_send()
        for k in range(1, n):
            rs_copy(lax.rem(me + k, n)).wait_send()

    if paired:
        finish_pairs()
    else:
        finish_direct()
    for cond, make in pending:

        @pl.when(cond)
        def _():
            make().wait_send()


def shards(inputs, cotangent, weights, tap_weights, projection, dilations):
    n, m = lax.axis_size("ctx"), lax.axis_size("dp")
    length, width = inputs.shape[1:]
    rows = weights.shape[1]
    tests = projection.shape[2]
    kr = tests // n
    tile = 256
    paired = m == 2 and width % (2 * tile) == 0
    pairs = width // (2 * tile) if paired else 1
    lead, wide = ((pairs,), tile) if paired else ((), width)
    hbm = pl.BlockSpec(memory_space=pltpu.HBM)
    vmem = pl.BlockSpec(memory_space=pltpu.VMEM)
    dma = pltpu.SemaphoreType.DMA
    grad, sketches = pl.pallas_call(
        functools.partial(kernel, n, m),
        out_shape=(
            jax.ShapeDtypeStruct((length, width // 2), BF16),
            jax.ShapeDtypeStruct((kr, width), F32),
        ),
        in_specs=[hbm, hbm, hbm, vmem, hbm, hbm],
        out_specs=(vmem, vmem),
        scratch_shapes=[
            pltpu.VMEM((length, width), BF16),
            pltpu.VMEM(projection.shape[1:], BF16),
            pltpu.SMEM(dilations.shape, jnp.int32),
            pltpu.VMEM((length, width), F32),
            pltpu.VMEM((length, width), F32),
            pltpu.VMEM((length, 128), F32),
            dma((5,)),
            pltpu.VMEM((n * rows, width), BF16),
            pltpu.VMEM((length, width), BF16),
            pltpu.VMEM((2 * DMAX, width), BF16),
            pltpu.VMEM((2 * DMAX, width), BF16),
            pltpu.VMEM((length, width), BF16),
            pltpu.VMEM((length, width), BF16),
            pltpu.VMEM((length, width), F32),
            pltpu.VMEM((length, width), BF16),
            pltpu.VMEM((length, width), BF16),
            pltpu.VMEM((length, width // 2), BF16),
            pltpu.VMEM(lead + (n, kr, wide), BF16),
            pltpu.VMEM(lead + (n, kr, wide), BF16),
            pltpu.VMEM((m,) + lead + (kr, wide), BF16),
            pltpu.VMEM((length, tests), BF16),
            pltpu.VMEM((pairs, n, kr, tile), BF16),
            pltpu.VMEM((pairs, n, kr, tile), BF16),
            pltpu.VMEM((pairs, n, kr, tile), F32),
            dma((n, 3, 5)),
            dma((n, 3)),
            dma((2, 2)),
            dma((2, 2)),
            dma((width // 256 + 2 * length // 64,)),
            dma((width // 256 + 2 * length // 64,)),
            dma(lead + (n,)),
            dma(lead + (n,)),
            dma(lead if paired else (m,)),
            dma(lead if paired else (m,)),
            dma((pairs,)),
            dma((pairs,)),
        ],
        compiler_params=pltpu.CompilerParams(
            collective_id=0, has_side_effects=True, vmem_limit_bytes=60 << 20
        ),
        name="segment",
    )(inputs, cotangent, weights, tap_weights[0], projection, dilations)
    return (grad[None], sketches[None])


def solution(mesh):
    in_specs = (
        P("dp", "ctx", None),
        P("dp", "ctx", None),
        P("segment", "ctx", None),
        P("segment", None, None),
        P("segment", None, None),
        P(),
    )
    out_specs = (P("dp", "ctx", "segment"), P("segment", "ctx", None))
    return jax.shard_map(shards, mesh=mesh, in_specs=in_specs, out_specs=out_specs, check_vma=False)
```

```python
import functools

import jax
import jax.numpy as jnp
from jax import lax
from jax.experimental import pallas as pl
from jax.experimental.pallas import tpu as pltpu
from jax.sharding import PartitionSpec as P

DMAX = 64
MESH = pl.DeviceIdType.MESH
F32 = jnp.float32
BF16 = jnp.bfloat16
ROOT = 0.7978845608028654
CUBIC = 0.044715


def line_width(n):
    width = 1
    while 4 * width * width <= n:
        width *= 2
    return width


def kernel(
    n, m, x_hbm, g_hbm, w_hbm, tap_ref, proj_hbm, dil_hbm, out_ref, sk_ref,
    io_ref, proj_ref, dil_ref, slope, normed, scale, l_sem, wf, act, halo_a, halo_g, mixed, gu, ga, first, second, other, sk, rs, dpb, pb, ys, yr, keep,
    w_send, w_recv, h_send, h_recv, c_send, c_recv, rs_send, rs_recv, dp_send, dp_recv,
    y_send, y_recv,
):
    me = lax.axis_index("ctx")
    dp = lax.axis_index("dp")
    seg = lax.axis_index("segment")
    length, width = io_ref.shape
    rows = w_hbm.shape[1]
    w_ref = w_hbm.at[0]
    kr = sk.shape[-2]
    X = line_width(n)
    Z = n // X
    z = me // X
    x = lax.rem(me, X)
    crossing = m % 2 == 0 and rows % 48 == 0
    parts = 2 if crossing else 1
    pr = rows // 3 if crossing else rows
    q = lax.rem(dp, 2) if crossing else 0

    own_rows = pl.ds(pl.multiple_of(me * rows, 16), rows)
    loads = [
        pltpu.make_async_copy(w_ref, wf.at[own_rows], l_sem.at[0]),
        pltpu.make_async_copy(proj_hbm.at[0], proj_ref, l_sem.at[1]),
        pltpu.make_async_copy(dil_hbm, dil_ref, l_sem.at[3]),
    ]

    @pl.when(seg == 0)
    def _():
        pltpu.make_async_copy(x_hbm.at[0], io_ref, l_sem.at[4]).start()

    @pl.when(seg == 1)
    def _():
        pltpu.make_async_copy(g_hbm.at[0], io_ref, l_sem.at[4]).start()

    for load in loads:
        load.start()

    order = (2 * q, 1)[:parts]

    barrier = pltpu.get_barrier_semaphore()
    for k in range(1, n):
        pl.semaphore_signal(barrier, inc=1, device_id={"ctx": lax.rem(me + k, n)}, device_id_type=MESH)
    for k in range(1, m):
        pl.semaphore_signal(barrier, inc=1, device_id={"dp": lax.rem(dp + k, m)}, device_id_type=MESH)
    pl.semaphore_signal(barrier, inc=1, device_id={"segment": 1 - seg}, device_id_type=MESH)
    pl.semaphore_wait(barrier, n + m - 1)

    def piece(block, part):
        return pl.ds(pl.multiple_of(block * rows + part * pr, 16), pr)

    def w_copy(block, part, direction, where, own=False):
        src = w_ref.at[pl.ds(pl.multiple_of(part * pr, 16), pr)] if own else wf.at[piece(block, part)]
        return pltpu.make_async_remote_copy(
            src_ref=src,
            dst_ref=wf.at[piece(block, part)],
            send_sem=w_send.at[block, part, direction],
            recv_sem=w_recv.at[block, part],
            device_id=where,
            device_id_type=MESH,
        )

    def sends_z(block, part, up, own=False):
        if up:
            return (z < Z - 1, lambda: w_copy(block, part, 0, {"ctx": me + X}, own))
        return (z > 0, lambda: w_copy(block, part, 1, {"ctx": me - X}, own))

    def sends_x(block, part, right, own=False):
        if right:
            return (x < X - 1, lambda: w_copy(block, part, 2, {"ctx": me + 1}, own))
        return (x > 0, lambda: w_copy(block, part, 3, {"ctx": me - 1}, own))

    pending = []

    def issue(guard, entry):
        cond, make = entry
        if guard is not None:
            cond = jnp.logical_and(guard, cond)

        @pl.when(cond)
        def _():
            make().start()

        pending.append((cond, make))

    def cross(guard, block, part):
        if crossing:
            cond = part == 2 * q
            if guard is not None:
                cond = jnp.logical_and(guard, cond)
            make = lambda: w_copy(block, part, 4, {"dp": dp + 1 - 2 * q})

            @pl.when(cond)
            def _():
                make().start()

            pending.append((cond, make))

    def arrived(guard, block, part):
        @pl.when(guard)
        def _():
            w_copy(block, part, 0, {"ctx": me}).wait_recv()

    def start_weights():
        for j in range(parts):
            for entry in (
                sends_z(me, order[j], True, True),
                sends_z(me, order[j], False, True),
                sends_x(me, order[j], True, True),
                sends_x(me, order[j], False, True),
            ):
                issue(None, entry)

    def spread_x(step):
        for t in range(1, X):
            for j in range(parts):
                part = order[j]
                for sign in (-1, 1):
                    for side in ((0,) if step == 0 else (-1, 1)):
                        zz = z + side * step
                        xx = x + sign * t
                        guard = functools.reduce(
                            jnp.logical_and, [zz >= 0, zz < Z, xx >= 0, xx < X]
                        )
                        block = jnp.clip(zz, 0, Z - 1) * X + jnp.clip(xx, 0, X - 1)
                        arrived(guard, block, part)
                        if t < X - 1:
                            issue(guard, sends_x(block, part, sign < 0))
                        cross(guard, block, part)

    def gather_weights(meanwhile):
        if Z == 1:
            meanwhile()
        for step in range(1, Z):
            for j in range(parts):
                part = order[j]
                for up in (True, False):
                    zz = z - step if up else z + step
                    guard = zz >= 0 if up else zz < Z
                    block = jnp.clip(zz, 0, Z - 1) * X + x
                    arrived(guard, block, part)
                    if step < Z - 1:
                        issue(guard, sends_z(block, part, up))
                    issue(guard, sends_x(block, part, True))
                    issue(guard, sends_x(block, part, False))
                    cross(guard, block, part)
            spread_x(step - 1)
            if step == 1:
                meanwhile()
        spread_x(Z - 1)
        if crossing:
            for k in range(1, n):
                block = lax.rem(me + k, n)
                w_copy(block, 2 - 2 * q, 4, {"dp": dp}).wait_recv()

    def halo_copies(which, src, dst):
        down = pltpu.make_async_remote_copy(
            src_ref=src.at[pl.ds(0, DMAX)], dst_ref=dst.at[pl.ds(DMAX, DMAX)],
            send_sem=h_send.at[which, 0], recv_sem=h_recv.at[which, 1],
            device_id={"ctx": me - 1}, device_id_type=MESH,
        )
        up = pltpu.make_async_remote_copy(
            src_ref=src.at[pl.ds(length - DMAX, DMAX)], dst_ref=dst.at[pl.ds(0, DMAX)],
            send_sem=h_send.at[which, 1], recv_sem=h_recv.at[which, 0],
            device_id={"ctx": me + 1}, device_id_type=MESH,
        )
        return down, up

    def start_halo(which, src, dst):
        down, up = halo_copies(which, src, dst)

        @pl.when(me > 0)
        def _():
            down.start()

        @pl.when(me == 0)
        def _():
            dst[pl.ds(0, DMAX), :] = jnp.zeros((DMAX, width), BF16)

        @pl.when(me < n - 1)
        def _():
            up.start()

        @pl.when(me == n - 1)
        def _():
            dst[pl.ds(DMAX, DMAX), :] = jnp.zeros((DMAX, width), BF16)

    def wait_halo(which, src, dst):
        down, up = halo_copies(which, src, dst)

        @pl.when(me > 0)
        def _():
            up.wait_recv()
            down.wait_send()

        @pl.when(me < n - 1)
        def _():
            down.wait_recv()
            up.wait_send()

    paired = len(sk.shape) == 4

    tile = 256

    def selectors():
        dilation = dil_ref[seg]
        t = lax.broadcasted_iota(jnp.int32, (length, length), 0)
        s = lax.broadcasted_iota(jnp.int32, (length, length), 1)
        th = lax.broadcasted_iota(jnp.int32, (length, 2 * DMAX), 0)
        h = lax.broadcasted_iota(jnp.int32, (length, 2 * DMAX), 1)
        one = lambda c: jnp.where(c, 1.0, 0.0).astype(BF16)
        before = (one(s == t - dilation), one((h - DMAX == th - dilation) & (h < DMAX)))
        after = (one(s == t + dilation), one((h - DMAX + length == th + dilation) & (h >= DMAX)))
        return before, after

    def convolve(src, halo, dst, flip):
        before, after = selectors()
        low, high = (2, 0) if flip else (0, 2)

        def body(c, carry):
            cols = pl.ds(pl.multiple_of(c * tile, tile), tile)
            own, edge = src[:, cols], halo[:, cols]
            pick = lambda sel: jnp.dot(sel[0], own, preferred_element_type=F32) + jnp.dot(
                sel[1], edge, preferred_element_type=F32
            )
            value = tap_ref[pl.ds(1, 1), cols] * own.astype(F32)
            value = tap_ref[pl.ds(low, 1), cols] * pick(before) + value
            value = value + tap_ref[pl.ds(high, 1), cols] * pick(after)
            dst[:, cols] = value.astype(dst.dtype)
            return carry

        lax.fori_loop(0, width // tile, body, 0)

    step_rows = 16

    def prepare(src):
        def body(i, carry):
            at = pl.ds(pl.multiple_of(i * step_rows, step_rows), step_rows)
            r = src[at, :].astype(F32)
            s = lax.rsqrt(jnp.mean(r * r, axis=-1, keepdims=True) + 1e-06)
            v = r * s
            vv = v * v
            t = jnp.tanh(ROOT * (v + CUBIC * (vv * v)))
            half = 0.5 * (1.0 + t)
            act[at, :] = (v * half).astype(BF16)
            slope[at, :] = half + 0.5 * v * (1.0 - t * t) * (ROOT * (1.0 + 3.0 * CUBIC * vv))
            normed[at, :] = v
            scale[at, :] = jnp.broadcast_to(s, (step_rows, 128))
            return carry

        lax.fori_loop(0, length // step_rows, body, 0)

    chunk = 64

    def pull_back(grad, store, send):
        def outer(c, carry):
            def body(i, carry):
                at = pl.ds(pl.multiple_of(c * chunk + i * step_rows, step_rows), step_rows)
                v = normed[at, :]
                s = scale[at, :][:, :1]
                dn = ga[at, :] * slope[at, :]
                gr = s * (dn - v * jnp.mean(dn * v, axis=-1, keepdims=True))
                store(at, grad[at, :].astype(F32) + gr)
                return carry

            lax.fori_loop(0, chunk // step_rows, body, 0)
            send(c).start()
            return carry

        lax.fori_loop(0, length // chunk, outer, 0)

    def project(grad):
        pb[...] = jnp.dot(grad[...], proj_ref[...], preferred_element_type=F32).astype(BF16)

    pairs = ys.shape[0]

    def y_copy(k):
        return pltpu.make_async_remote_copy(
            src_ref=ys.at[k], dst_ref=yr.at[k], send_sem=y_send.at[k], recv_sem=y_recv.at[k],
            device_id={"dp": 1 - dp}, device_id_type=MESH,
        )

    def sketch_tile(c):
        cols = pl.ds(pl.multiple_of(c * tile, tile), tile)
        return lax.dot_general(
            pb[...], mixed[:, cols], (((0,), (0,)), ((), ())), preferred_element_type=F32
        )

    def sketch_pairs():
        def body(k, carry):
            value = sketch_tile(2 * k + 1 - dp).astype(BF16)
            for b in range(n):
                ys[k, b] = value[b * kr : (b + 1) * kr]
            y_copy(k).start()
            return carry

        lax.fori_loop(0, pairs, body, 0)

        def mine(k, carry):
            value = sketch_tile(2 * k + dp)
            for b in range(n):
                keep[k, b] = value[b * kr : (b + 1) * kr]
            return carry

        lax.fori_loop(0, pairs, mine, 0)

    def c_copy(k, peer, slot):
        return pltpu.make_async_remote_copy(
            src_ref=sk.at[k, peer], dst_ref=rs.at[k, slot], send_sem=rs_send.at[k, peer],
            recv_sem=rs_recv.at[k, slot], device_id={"ctx": peer}, device_id_type=MESH,
        )

    def spread_pairs():
        def body(k, carry):
            y_copy(k).wait_recv()
            sk[k] = (keep[k] + yr[k].astype(F32)).astype(BF16)
            for j in range(1, n):
                c_copy(k, lax.rem(me + j, n), me).start()
            return carry

        lax.fori_loop(0, pairs, body, 0)

    def d_copy(k, slot):
        return pltpu.make_async_remote_copy(
            src_ref=dpb.at[slot, k], dst_ref=dpb.at[slot, k], send_sem=dp_send.at[k],
            recv_sem=dp_recv.at[k], device_id={"dp": 1 - dp}, device_id_type=MESH,
        )

    def finish_pairs():
        def body(k, carry):
            total = sk[k, me].astype(F32)
            for j in range(1, n):
                peer = lax.rem(me + j, n)
                c_copy(k, peer, peer).wait_recv()
                total = total + rs[k, peer].astype(F32)
            dpb[dp, k] = total.astype(BF16)
            d_copy(k, dp).start()
            return carry

        lax.fori_loop(0, pairs, body, 0)
        for k in range(pairs):
            d_copy(k, 1 - dp).wait_recv()
            for slot in range(2):
                c = 2 * k + slot
                sk_ref[:, c * tile : (c + 1) * tile] = dpb[slot, k].astype(F32)
        for k in range(pairs):
            d_copy(k, dp).wait_send()
            y_copy(k).wait_send()
            for j in range(1, n):
                c_copy(k, lax.rem(me + j, n), me).wait_send()

    def sketch():
        if paired:
            return sketch_pairs()
        def body(c, carry):
            cols = pl.ds(pl.multiple_of(c * tile, tile), tile)
            value = lax.dot_general(
                pb[...], mixed[:, cols], (((0,), (0,)), ((), ())), preferred_element_type=F32
            ).astype(BF16)
            for k in range(n):
                sk[k, :, cols] = value[k * kr : (k + 1) * kr]
            return carry

        lax.fori_loop(0, width // tile, body, 0)
        for k in range(1, n):
            rs_copy(lax.rem(me + k, n)).start()

    def rs_copy(peer):
        return pltpu.make_async_remote_copy(
            src_ref=sk.at[peer], dst_ref=rs.at[me],
            send_sem=rs_send.at[peer], recv_sem=rs_recv.at[me],
            device_id={"ctx": peer}, device_id_type=MESH,
        )

    def back_product(grad):
        def body(c, carry):
            cols = pl.ds(pl.multiple_of(c * tile, tile), tile)
            gu[:, cols] = lax.dot_general(
                grad[...], wf[cols, :], (((1,), (1,)), ((), ())), preferred_element_type=F32
            ).astype(BF16)
            return carry

        lax.fori_loop(0, width // tile, body, 0)

    def core_copy(index, src, dst):
        return pltpu.make_async_remote_copy(
            src_ref=src, dst_ref=dst, send_sem=c_send.at[index], recv_sem=c_recv.at[index],
            device_id={"segment": 1 - seg}, device_id_type=MESH,
        )

    half = width // 2
    tiles, chunks = width // tile, length // chunk

    def mid_copy(c):
        cols = pl.ds(pl.multiple_of(c * tile, tile), tile)
        return core_copy(c, first.at[:, cols], second.at[:, cols])

    def back_copy(c):
        at = pl.ds(pl.multiple_of(c * chunk, chunk), chunk)
        return core_copy(tiles + c, first.at[at], second.at[at])

    def half_copy(c):
        at = pl.ds(pl.multiple_of(c * chunk, chunk), chunk)
        return core_copy(tiles + chunks + c, other.at[at], out_ref.at[at])

    start_weights()
    pltpu.make_async_copy(x_hbm.at[0], io_ref, l_sem.at[4]).wait()
    for load in loads:
        load.wait()

    @pl.when(seg == 0)
    def _():
        prepare(io_ref)
        start_halo(0, act, halo_a)

    @pl.when(seg == 1)
    def _():
        project(io_ref)

    def mix_first():
        @pl.when(seg == 0)
        def _():
            wait_halo(0, act, halo_a)
            convolve(act, halo_a, mixed, False)

    gather_weights(mix_first)

    @pl.when(seg == 0)
    def _():
        def body(c, carry):
            cols = pl.ds(pl.multiple_of(c * tile, tile), tile)
            value = jnp.dot(mixed[...], wf[:, cols], preferred_element_type=F32)
            first[:, cols] = (io_ref[:, cols].astype(F32) + value).astype(BF16)
            mid_copy(c).start()
            return carry

        lax.fori_loop(0, tiles, body, 0)
        for c in range(tiles):
            mid_copy(c).wait_send()
        for c in range(chunks):
            back_copy(c).wait_recv()
        project(second)
        sketch()
        back_product(second)
        start_halo(1, gu, halo_g)
        if paired:
            spread_pairs()
        wait_halo(1, gu, halo_g)
        convolve(gu, halo_g, ga, True)

        def store(at, grad):
            out_ref[at, :] = grad[:, :half].astype(BF16)
            other[at, :] = grad[:, half:].astype(BF16)

        pull_back(second, store, half_copy)
        for c in range(chunks):
            half_copy(c).wait_send()

    @pl.when(seg == 1)
    def _():
        back_product(io_ref)
        start_halo(1, gu, halo_g)
        for c in range(tiles):
            mid_copy(c).wait_recv()
        prepare(second)
        start_halo(0, act, halo_a)
        wait_halo(1, gu, halo_g)
        convolve(gu, halo_g, ga, True)

        def store(at, grad):
            first[at, :] = grad.astype(BF16)

        pull_back(io_ref, store, back_copy)
        wait_halo(0, act, halo_a)
        convolve(act, halo_a, mixed, False)
        sketch()
        if paired:
            spread_pairs()
        for c in range(chunks):
            back_copy(c).wait_send()
        for c in range(chunks):
            half_copy(c).wait_recv()

    def finish_direct():
        total = sk[me].astype(F32)
        for k in range(1, n):
            peer = lax.rem(me + k, n)
            pltpu.make_async_remote_copy(
                src_ref=sk.at[peer], dst_ref=rs.at[peer], send_sem=rs_send.at[peer],
                recv_sem=rs_recv.at[peer], device_id={"ctx": peer}, device_id_type=MESH,
            ).wait_recv()
            total = total + rs[peer].astype(F32)
        dpb[dp] = total.astype(BF16)

        def dp_copy(peer, slot):
            return pltpu.make_async_remote_copy(
                src_ref=dpb.at[slot], dst_ref=dpb.at[slot], send_sem=dp_send.at[peer],
                recv_sem=dp_recv.at[slot], device_id={"dp": peer}, device_id_type=MESH,
            )

        for k in range(1, m):
            dp_copy(lax.rem(dp + k, m), dp).start()
        for k in range(1, m):
            dp_copy(lax.rem(dp + k, m), lax.rem(dp + k, m)).wait_recv()
        merged = dpb[0].astype(F32)
        for k in range(1, m):
            merged = merged + dpb[k].astype(F32)
        sk_ref[...] = merged

        for k in range(1, m):
            dp_copy(lax.rem(dp + k, m), dp).wait_send()
        for k in range(1, n):
            rs_copy(lax.rem(me + k, n)).wait_send()

    if paired:
        finish_pairs()
    else:
        finish_direct()
    for cond, make in pending:

        @pl.when(cond)
        def _():
            make().wait_send()


def shards(inputs, cotangent, weights, tap_weights, projection, dilations):
    n, m = lax.axis_size("ctx"), lax.axis_size("dp")
    length, width = inputs.shape[1:]
    rows = weights.shape[1]
    tests = projection.shape[2]
    kr = tests // n
    tile = 256
    paired = m == 2 and width % (2 * tile) == 0
    pairs = width // (2 * tile) if paired else 1
    lead, wide = ((pairs,), tile) if paired else ((), width)
    hbm = pl.BlockSpec(memory_space=pltpu.HBM)
    vmem = pl.BlockSpec(memory_space=pltpu.VMEM)
    dma = pltpu.SemaphoreType.DMA
    grad, sketches = pl.pallas_call(
        functools.partial(kernel, n, m),
        out_shape=(
            jax.ShapeDtypeStruct((length, width // 2), BF16),
            jax.ShapeDtypeStruct((kr, width), F32),
        ),
        in_specs=[hbm, hbm, hbm, vmem, hbm, hbm],
        out_specs=(vmem, vmem),
        scratch_shapes=[
            pltpu.VMEM((length, width), BF16),
            pltpu.VMEM(projection.shape[1:], BF16),
            pltpu.SMEM(dilations.shape, jnp.int32),
            pltpu.VMEM((length, width), F32),
            pltpu.VMEM((length, width), F32),
            pltpu.VMEM((length, 128), F32),
            dma((5,)),
            pltpu.VMEM((n * rows, width), BF16),
            pltpu.VMEM((length, width), BF16),
            pltpu.VMEM((2 * DMAX, width), BF16),
            pltpu.VMEM((2 * DMAX, width), BF16),
            pltpu.VMEM((length, width), BF16),
            pltpu.VMEM((length, width), BF16),
            pltpu.VMEM((length, width), F32),
            pltpu.VMEM((length, width), BF16),
            pltpu.VMEM((length, width), BF16),
            pltpu.VMEM((length, width // 2), BF16),
            pltpu.VMEM(lead + (n, kr, wide), BF16),
            pltpu.VMEM(lead + (n, kr, wide), BF16),
            pltpu.VMEM((m,) + lead + (kr, wide), BF16),
            pltpu.VMEM((length, tests), BF16),
            pltpu.VMEM((pairs, n, kr, tile), BF16),
            pltpu.VMEM((pairs, n, kr, tile), BF16),
            pltpu.VMEM((pairs, n, kr, tile), F32),
            dma((n, 3, 5)),
            dma((n, 3)),
            dma((2, 2)),
            dma((2, 2)),
            dma((width // 256 + 2 * length // 64,)),
            dma((width // 256 + 2 * length // 64,)),
            dma(lead + (n,)),
            dma(lead + (n,)),
            dma(lead if paired else (m,)),
            dma(lead if paired else (m,)),
            dma((pairs,)),
            dma((pairs,)),
        ],
        compiler_params=pltpu.CompilerParams(
            collective_id=0, has_side_effects=True, vmem_limit_bytes=60 << 20
        ),
        name="segment",
    )(inputs, cotangent, weights, tap_weights[0], projection, dilations)
    return (grad[None], sketches[None])


def solution(mesh):
    in_specs = (
        P("dp", "ctx", None),
        P("dp", "ctx", None),
        P("segment", "ctx", None),
        P("segment", None, None),
        P("segment", None, None),
        P(),
    )
    out_specs = (P("dp", "ctx", "segment"), P("segment", "ctx", None))
    return jax.shard_map(shards, mesh=mesh, in_specs=in_specs, out_specs=out_specs, check_vma=False)
```

```python
import functools

import jax
import jax.numpy as jnp
from jax import lax
from jax.experimental import pallas as pl
from jax.experimental.pallas import tpu as pltpu
from jax.sharding import PartitionSpec as P

DMAX = 64
MESH = pl.DeviceIdType.MESH
F32 = jnp.float32
BF16 = jnp.bfloat16
ROOT = 0.7978845608028654
CUBIC = 0.044715


def line_width(n):
    width = 1
    while 4 * width * width <= n:
        width *= 2
    return width


def kernel(
    n, m, x_hbm, g_hbm, w_hbm, tap_ref, proj_hbm, dil_hbm, out_ref, sk_ref,
    io_ref, proj_ref, dil_ref, slope, normed, scale, l_sem, wf, act, halo_a, halo_g, mixed, gu, ga, first, second, other, sk, rs, dpb, pb, ys, yr, keep,
    w_send, w_recv, h_send, h_recv, c_send, c_recv, rs_send, rs_recv, dp_send, dp_recv,
    y_send, y_recv,
):
    me = lax.axis_index("ctx")
    dp = lax.axis_index("dp")
    seg = lax.axis_index("segment")
    length, width = io_ref.shape
    rows = w_hbm.shape[1]
    w_ref = w_hbm.at[0]
    kr = sk.shape[-2]
    X = line_width(n)
    Z = n // X
    z = me // X
    x = lax.rem(me, X)
    crossing = m % 2 == 0 and rows % 48 == 0
    parts = 2 if crossing else 1
    pr = rows // 3 if crossing else rows
    q = lax.rem(dp, 2) if crossing else 0

    own_rows = pl.ds(pl.multiple_of(me * rows, 16), rows)
    loads = [
        pltpu.make_async_copy(w_ref, wf.at[own_rows], l_sem.at[0]),
        pltpu.make_async_copy(proj_hbm.at[0], proj_ref, l_sem.at[1]),
        pltpu.make_async_copy(dil_hbm, dil_ref, l_sem.at[3]),
    ]

    @pl.when(seg == 0)
    def _():
        pltpu.make_async_copy(x_hbm.at[0], io_ref, l_sem.at[4]).start()

    @pl.when(seg == 1)
    def _():
        pltpu.make_async_copy(g_hbm.at[0], io_ref, l_sem.at[4]).start()

    for load in loads:
        load.start()

    shift = crossing and X == 2 and Z > 1
    order = (2 * q, 1)[:parts]

    barrier = pltpu.get_barrier_semaphore()
    for k in range(1, n):
        pl.semaphore_signal(barrier, inc=1, device_id={"ctx": lax.rem(me + k, n)}, device_id_type=MESH)
    for k in range(1, m):
        pl.semaphore_signal(barrier, inc=1, device_id={"dp": lax.rem(dp + k, m)}, device_id_type=MESH)
    pl.semaphore_signal(barrier, inc=1, device_id={"segment": 1 - seg}, device_id_type=MESH)
    pl.semaphore_wait(barrier, n + m - 1)

    def piece(block, part):
        return pl.ds(pl.multiple_of(block * rows + part * pr, 16), pr)

    def w_copy(block, part, direction, where, own=False):
        src = w_ref.at[pl.ds(pl.multiple_of(part * pr, 16), pr)] if own else wf.at[piece(block, part)]
        return pltpu.make_async_remote_copy(
            src_ref=src,
            dst_ref=wf.at[piece(block, part)],
            send_sem=w_send.at[block, part, direction],
            recv_sem=w_recv.at[block, part],
            device_id=where,
            device_id_type=MESH,
        )

    def sends_z(block, part, up, own=False):
        if up:
            return (z < Z - 1, lambda: w_copy(block, part, 0, {"ctx": me + X}, own))
        return (z > 0, lambda: w_copy(block, part, 1, {"ctx": me - X}, own))

    def sends_x(block, part, right, own=False):
        if right:
            return (x < X - 1, lambda: w_copy(block, part, 2, {"ctx": me + 1}, own))
        return (x > 0, lambda: w_copy(block, part, 3, {"ctx": me - 1}, own))

    pending = []

    def issue(guard, entry):
        cond, make = entry
        if guard is not None:
            cond = jnp.logical_and(guard, cond)

        @pl.when(cond)
        def _():
            make().start()

        pending.append((cond, make))

    def cross(guard, block, part):
        if crossing:
            cond = part == 2 * q
            if guard is not None:
                cond = jnp.logical_and(guard, cond)
            make = lambda: w_copy(block, part, 4, {"dp": dp + 1 - 2 * q})

            @pl.when(cond)
            def _():
                make().start()

            pending.append((cond, make))

    def arrived(guard, block, part):
        @pl.when(guard)
        def _():
            w_copy(block, part, 0, {"ctx": me}).wait_recv()

    def start_weights():
        for j in range(parts):
            for entry in (
                sends_z(me, order[j], True, True),
                sends_z(me, order[j], False, True),
                sends_x(me, order[j], True, True),
                sends_x(me, order[j], False, True),
            ):
                issue(None, entry)

    def spread_x(step):
        for t in range(1, X):
            for j in range(parts):
                part = order[j]
                for sign in (-1, 1):
                    for side in ((0,) if step == 0 else (-1, 1)):
                        zz = z + side * step
                        xx = x + sign * t
                        guard = functools.reduce(
                            jnp.logical_and, [zz >= 0, zz < Z, xx >= 0, xx < X]
                        )
                        block = jnp.clip(zz, 0, Z - 1) * X + jnp.clip(xx, 0, X - 1)
                        arrived(guard, block, part)
                        if t < X - 1:
                            issue(guard, sends_x(block, part, sign < 0))
                        if shift and j == 1:
                            for up in ((True, False) if step == 0 else (side < 0,)):
                                end = zz == (0 if up else Z - 1)
                                issue(jnp.logical_and(guard, end), sends_z(block, part, up))
                        cross(guard, block, part)

    def gather_weights(meanwhile):
        if Z == 1:
            meanwhile()
        for step in range(1, Z):
            for j in range(parts):
                part = order[j]
                for up in (True, False):
                    zz = z - step if up else z + step
                    guard = zz >= 0 if up else zz < Z
                    block = jnp.clip(zz, 0, Z - 1) * X + x
                    arrived(guard, block, part)
                    if step < Z - 1:
                        issue(guard, sends_z(block, part, up))
                    inner = guard
                    if shift and j == 1:
                        inner = jnp.logical_and(guard, zz != (0 if up else Z - 1))
                    issue(inner, sends_x(block, part, True))
                    issue(inner, sends_x(block, part, False))
                    cross(guard, block, part)
            spread_x(step - 1)
            if step == 1:
                meanwhile()
        spread_x(Z - 1)
        if crossing:
            for k in range(1, n):
                block = lax.rem(me + k, n)
                w_copy(block, 2 - 2 * q, 4, {"dp": dp}).wait_recv()

    def halo_copies(which, src, dst):
        down = pltpu.make_async_remote_copy(
            src_ref=src.at[pl.ds(0, DMAX)], dst_ref=dst.at[pl.ds(DMAX, DMAX)],
            send_sem=h_send.at[which, 0], recv_sem=h_recv.at[which, 1],
            device_id={"ctx": me - 1}, device_id_type=MESH,
        )
        up = pltpu.make_async_remote_copy(
            src_ref=src.at[pl.ds(length - DMAX, DMAX)], dst_ref=dst.at[pl.ds(0, DMAX)],
            send_sem=h_send.at[which, 1], recv_sem=h_recv.at[which, 0],
            device_id={"ctx": me + 1}, device_id_type=MESH,
        )
        return down, up

    def start_halo(which, src, dst):
        down, up = halo_copies(which, src, dst)

        @pl.when(me > 0)
        def _():
            down.start()

        @pl.when(me == 0)
        def _():
            dst[pl.ds(0, DMAX), :] = jnp.zeros((DMAX, width), BF16)

        @pl.when(me < n - 1)
        def _():
            up.start()

        @pl.when(me == n - 1)
        def _():
            dst[pl.ds(DMAX, DMAX), :] = jnp.zeros((DMAX, width), BF16)

    def wait_halo(which, src, dst):
        down, up = halo_copies(which, src, dst)

        @pl.when(me > 0)
        def _():
            up.wait_recv()
            down.wait_send()

        @pl.when(me < n - 1)
        def _():
            down.wait_recv()
            up.wait_send()

    paired = len(sk.shape) == 4

    tile = 256

    def selectors():
        dilation = dil_ref[seg]
        t = lax.broadcasted_iota(jnp.int32, (length, length), 0)
        s = lax.broadcasted_iota(jnp.int32, (length, length), 1)
        th = lax.broadcasted_iota(jnp.int32, (length, 2 * DMAX), 0)
        h = lax.broadcasted_iota(jnp.int32, (length, 2 * DMAX), 1)
        one = lambda c: jnp.where(c, 1.0, 0.0).astype(BF16)
        before = (one(s == t - dilation), one((h - DMAX == th - dilation) & (h < DMAX)))
        after = (one(s == t + dilation), one((h - DMAX + length == th + dilation) & (h >= DMAX)))
        return before, after

    def convolve(src, halo, dst, flip):
        before, after = selectors()
        low, high = (2, 0) if flip else (0, 2)

        def body(c, carry):
            cols = pl.ds(pl.multiple_of(c * tile, tile), tile)
            own, edge = src[:, cols], halo[:, cols]
            pick = lambda sel: jnp.dot(sel[0], own, preferred_element_type=F32) + jnp.dot(
                sel[1], edge, preferred_element_type=F32
            )
            value = tap_ref[pl.ds(1, 1), cols] * own.astype(F32)
            value = tap_ref[pl.ds(low, 1), cols] * pick(before) + value
            value = value + tap_ref[pl.ds(high, 1), cols] * pick(after)
            dst[:, cols] = value.astype(dst.dtype)
            return carry

        lax.fori_loop(0, width // tile, body, 0)

    step_rows = 16

    def prepare(src):
        def body(i, carry):
            at = pl.ds(pl.multiple_of(i * step_rows, step_rows), step_rows)
            r = src[at, :].astype(F32)
            s = lax.rsqrt(jnp.mean(r * r, axis=-1, keepdims=True) + 1e-06)
            v = r * s
            vv = v * v
            t = jnp.tanh(ROOT * (v + CUBIC * (vv * v)))
            half = 0.5 * (1.0 + t)
            act[at, :] = (v * half).astype(BF16)
            slope[at, :] = half + 0.5 * v * (1.0 - t * t) * (ROOT * (1.0 + 3.0 * CUBIC * vv))
            normed[at, :] = v
            scale[at, :] = jnp.broadcast_to(s, (step_rows, 128))
            return carry

        lax.fori_loop(0, length // step_rows, body, 0)

    chunk = 64

    def pull_back(grad, store, send):
        def outer(c, carry):
            def body(i, carry):
                at = pl.ds(pl.multiple_of(c * chunk + i * step_rows, step_rows), step_rows)
                v = normed[at, :]
                s = scale[at, :][:, :1]
                dn = ga[at, :] * slope[at, :]
                gr = s * (dn - v * jnp.mean(dn * v, axis=-1, keepdims=True))
                store(at, grad[at, :].astype(F32) + gr)
                return carry

            lax.fori_loop(0, chunk // step_rows, body, 0)
            send(c).start()
            return carry

        lax.fori_loop(0, length // chunk, outer, 0)

    def project(grad):
        pb[...] = jnp.dot(grad[...], proj_ref[...], preferred_element_type=F32).astype(BF16)

    pairs = ys.shape[0]

    def y_copy(k):
        return pltpu.make_async_remote_copy(
            src_ref=ys.at[k], dst_ref=yr.at[k], send_sem=y_send.at[k], recv_sem=y_recv.at[k],
            device_id={"dp": 1 - dp}, device_id_type=MESH,
        )

    def sketch_tile(c):
        cols = pl.ds(pl.multiple_of(c * tile, tile), tile)
        return lax.dot_general(
            pb[...], mixed[:, cols], (((0,), (0,)), ((), ())), preferred_element_type=F32
        )

    def sketch_pairs():
        def body(k, carry):
            value = sketch_tile(2 * k + 1 - dp).astype(BF16)
            for b in range(n):
                ys[k, b] = value[b * kr : (b + 1) * kr]
            y_copy(k).start()
            return carry

        lax.fori_loop(0, pairs, body, 0)

        def mine(k, carry):
            value = sketch_tile(2 * k + dp)
            for b in range(n):
                keep[k, b] = value[b * kr : (b + 1) * kr]
            return carry

        lax.fori_loop(0, pairs, mine, 0)

    def c_copy(k, peer, slot):
        return pltpu.make_async_remote_copy(
            src_ref=sk.at[k, peer], dst_ref=rs.at[k, slot], send_sem=rs_send.at[k, peer],
            recv_sem=rs_recv.at[k, slot], device_id={"ctx": peer}, device_id_type=MESH,
        )

    def spread_pairs():
        def body(k, carry):
            y_copy(k).wait_recv()
            sk[k] = (keep[k] + yr[k].astype(F32)).astype(BF16)
            for j in range(1, n):
                c_copy(k, lax.rem(me + j, n), me).start()
            return carry

        lax.fori_loop(0, pairs, body, 0)

    def d_copy(k, slot):
        return pltpu.make_async_remote_copy(
            src_ref=dpb.at[slot, k], dst_ref=dpb.at[slot, k], send_sem=dp_send.at[k],
            recv_sem=dp_recv.at[k], device_id={"dp": 1 - dp}, device_id_type=MESH,
        )

    def finish_pairs():
        def body(k, carry):
            total = sk[k, me].astype(F32)
            for j in range(1, n):
                peer = lax.rem(me + j, n)
                c_copy(k, peer, peer).wait_recv()
                total = total + rs[k, peer].astype(F32)
            dpb[dp, k] = total.astype(BF16)
            d_copy(k, dp).start()
            return carry

        lax.fori_loop(0, pairs, body, 0)
        for k in range(pairs):
            d_copy(k, 1 - dp).wait_recv()
            for slot in range(2):
                c = 2 * k + slot
                sk_ref[:, c * tile : (c + 1) * tile] = dpb[slot, k].astype(F32)
        for k in range(pairs):
            d_copy(k, dp).wait_send()
            y_copy(k).wait_send()
            for j in range(1, n):
                c_copy(k, lax.rem(me + j, n), me).wait_send()

    def sketch():
        if paired:
            return sketch_pairs()
        def body(c, carry):
            cols = pl.ds(pl.multiple_of(c * tile, tile), tile)
            value = lax.dot_general(
                pb[...], mixed[:, cols], (((0,), (0,)), ((), ())), preferred_element_type=F32
            ).astype(BF16)
            for k in range(n):
                sk[k, :, cols] = value[k * kr : (k + 1) * kr]
            return carry

        lax.fori_loop(0, width // tile, body, 0)
        for k in range(1, n):
            rs_copy(lax.rem(me + k, n)).start()

    def rs_copy(peer):
        return pltpu.make_async_remote_copy(
            src_ref=sk.at[peer], dst_ref=rs.at[me],
            send_sem=rs_send.at[peer], recv_sem=rs_recv.at[me],
            device_id={"ctx": peer}, device_id_type=MESH,
        )

    def back_product(grad):
        def body(c, carry):
            cols = pl.ds(pl.multiple_of(c * tile, tile), tile)
            gu[:, cols] = lax.dot_general(
                grad[...], wf[cols, :], (((1,), (1,)), ((), ())), preferred_element_type=F32
            ).astype(BF16)
            return carry

        lax.fori_loop(0, width // tile, body, 0)

    def core_copy(index, src, dst):
        return pltpu.make_async_remote_copy(
            src_ref=src, dst_ref=dst, send_sem=c_send.at[index], recv_sem=c_recv.at[index],
            device_id={"segment": 1 - seg}, device_id_type=MESH,
        )

    half = width // 2
    tiles, chunks = width // tile, length // chunk

    def mid_copy(c):
        cols = pl.ds(pl.multiple_of(c * tile, tile), tile)
        return core_copy(c, first.at[:, cols], second.at[:, cols])

    def back_copy(c):
        at = pl.ds(pl.multiple_of(c * chunk, chunk), chunk)
        return core_copy(tiles + c, first.at[at], second.at[at])

    def half_copy(c):
        at = pl.ds(pl.multiple_of(c * chunk, chunk), chunk)
        return core_copy(tiles + chunks + c, other.at[at], out_ref.at[at])

    start_weights()
    pltpu.make_async_copy(x_hbm.at[0], io_ref, l_sem.at[4]).wait()
    for load in loads:
        load.wait()

    @pl.when(seg == 0)
    def _():
        prepare(io_ref)
        start_halo(0, act, halo_a)

    @pl.when(seg == 1)
    def _():
        project(io_ref)

    def mix_first():
        @pl.when(seg == 0)
        def _():
            wait_halo(0, act, halo_a)
            convolve(act, halo_a, mixed, False)

    gather_weights(mix_first)

    @pl.when(seg == 0)
    def _():
        def body(c, carry):
            cols = pl.ds(pl.multiple_of(c * tile, tile), tile)
            value = jnp.dot(mixed[...], wf[:, cols], preferred_element_type=F32)
            first[:, cols] = (io_ref[:, cols].astype(F32) + value).astype(BF16)
            mid_copy(c).start()
            return carry

        lax.fori_loop(0, tiles, body, 0)
        for c in range(tiles):
            mid_copy(c).wait_send()
        for c in range(chunks):
            back_copy(c).wait_recv()
        project(second)
        sketch()
        back_product(second)
        start_halo(1, gu, halo_g)
        if paired:
            spread_pairs()
        wait_halo(1, gu, halo_g)
        convolve(gu, halo_g, ga, True)

        def store(at, grad):
            out_ref[at, :] = grad[:, :half].astype(BF16)
            other[at, :] = grad[:, half:].astype(BF16)

        pull_back(second, store, half_copy)
        for c in range(chunks):
            half_copy(c).wait_send()

    @pl.when(seg == 1)
    def _():
        back_product(io_ref)
        start_halo(1, gu, halo_g)
        for c in range(tiles):
            mid_copy(c).wait_recv()
        prepare(second)
        start_halo(0, act, halo_a)
        wait_halo(1, gu, halo_g)
        convolve(gu, halo_g, ga, True)

        def store(at, grad):
            first[at, :] = grad.astype(BF16)

        pull_back(io_ref, store, back_copy)
        wait_halo(0, act, halo_a)
        convolve(act, halo_a, mixed, False)
        sketch()
        if paired:
            spread_pairs()
        for c in range(chunks):
            back_copy(c).wait_send()
        for c in range(chunks):
            half_copy(c).wait_recv()

    def finish_direct():
        total = sk[me].astype(F32)
        for k in range(1, n):
            peer = lax.rem(me + k, n)
            pltpu.make_async_remote_copy(
                src_ref=sk.at[peer], dst_ref=rs.at[peer], send_sem=rs_send.at[peer],
                recv_sem=rs_recv.at[peer], device_id={"ctx": peer}, device_id_type=MESH,
            ).wait_recv()
            total = total + rs[peer].astype(F32)
        dpb[dp] = total.astype(BF16)

        def dp_copy(peer, slot):
            return pltpu.make_async_remote_copy(
                src_ref=dpb.at[slot], dst_ref=dpb.at[slot], send_sem=dp_send.at[peer],
                recv_sem=dp_recv.at[slot], device_id={"dp": peer}, device_id_type=MESH,
            )

        for k in range(1, m):
            dp_copy(lax.rem(dp + k, m), dp).start()
        for k in range(1, m):
            dp_copy(lax.rem(dp + k, m), lax.rem(dp + k, m)).wait_recv()
        merged = dpb[0].astype(F32)
        for k in range(1, m):
            merged = merged + dpb[k].astype(F32)
        sk_ref[...] = merged

        for k in range(1, m):
            dp_copy(lax.rem(dp + k, m), dp).wait_send()
        for k in range(1, n):
            rs_copy(lax.rem(me + k, n)).wait_send()

    if paired:
        finish_pairs()
    else:
        finish_direct()
    for cond, make in pending:

        @pl.when(cond)
        def _():
            make().wait_send()


def shards(inputs, cotangent, weights, tap_weights, projection, dilations):
    n, m = lax.axis_size("ctx"), lax.axis_size("dp")
    length, width = inputs.shape[1:]
    rows = weights.shape[1]
    tests = projection.shape[2]
    kr = tests // n
    tile = 256
    paired = m == 2 and width % (2 * tile) == 0
    pairs = width // (2 * tile) if paired else 1
    lead, wide = ((pairs,), tile) if paired else ((), width)
    hbm = pl.BlockSpec(memory_space=pltpu.HBM)
    vmem = pl.BlockSpec(memory_space=pltpu.VMEM)
    dma = pltpu.SemaphoreType.DMA
    grad, sketches = pl.pallas_call(
        functools.partial(kernel, n, m),
        out_shape=(
            jax.ShapeDtypeStruct((length, width // 2), BF16),
            jax.ShapeDtypeStruct((kr, width), F32),
        ),
        in_specs=[hbm, hbm, hbm, vmem, hbm, hbm],
        out_specs=(vmem, vmem),
        scratch_shapes=[
            pltpu.VMEM((length, width), BF16),
            pltpu.VMEM(projection.shape[1:], BF16),
            pltpu.SMEM(dilations.shape, jnp.int32),
            pltpu.VMEM((length, width), F32),
            pltpu.VMEM((length, width), F32),
            pltpu.VMEM((length, 128), F32),
            dma((5,)),
            pltpu.VMEM((n * rows, width), BF16),
            pltpu.VMEM((length, width), BF16),
            pltpu.VMEM((2 * DMAX, width), BF16),
            pltpu.VMEM((2 * DMAX, width), BF16),
            pltpu.VMEM((length, width), BF16),
            pltpu.VMEM((length, width), BF16),
            pltpu.VMEM((length, width), F32),
            pltpu.VMEM((length, width), BF16),
            pltpu.VMEM((length, width), BF16),
            pltpu.VMEM((length, width // 2), BF16),
            pltpu.VMEM(lead + (n, kr, wide), BF16),
            pltpu.VMEM(lead + (n, kr, wide), BF16),
            pltpu.VMEM((m,) + lead + (kr, wide), BF16),
            pltpu.VMEM((length, tests), BF16),
            pltpu.VMEM((pairs, n, kr, tile), BF16),
            pltpu.VMEM((pairs, n, kr, tile), BF16),
            pltpu.VMEM((pairs, n, kr, tile), F32),
            dma((n, 3, 5)),
            dma((n, 3)),
            dma((2, 2)),
            dma((2, 2)),
            dma((width // 256 + 2 * length // 64,)),
            dma((width // 256 + 2 * length // 64,)),
            dma(lead + (n,)),
            dma(lead + (n,)),
            dma(lead if paired else (m,)),
            dma(lead if paired else (m,)),
            dma((pairs,)),
            dma((pairs,)),
        ],
        compiler_params=pltpu.CompilerParams(
            collective_id=0, has_side_effects=True, vmem_limit_bytes=60 << 20
        ),
        name="segment",
    )(inputs, cotangent, weights, tap_weights[0], projection, dilations)
    return (grad[None], sketches[None])


def solution(mesh):
    in_specs = (
        P("dp", "ctx", None),
        P("dp", "ctx", None),
        P("segment", "ctx", None),
        P("segment", None, None),
        P("segment", None, None),
        P(),
    )
    out_specs = (P("dp", "ctx", "segment"), P("segment", "ctx", None))
    return jax.shard_map(shards, mesh=mesh, in_specs=in_specs, out_specs=out_specs, check_vma=False)
```
